32 devices in a mesh: grid: 8 (over y, x, core), sens: 4 (over z).
Axes of the slice: x: 2, y: 2, z: 4, core: 2. Of those that a mesh axis runs over, the one named last changes fastest.
Arguments:
- records: float32 [8, 128, 2048], P('grid', 'sens'), may hold values from -400 to 400
- travel_p: int32 [8, 128, 1024], P(None, 'sens', 'grid'), may hold values from 0 to 63
- travel_s: int32 [8, 128, 1024], P(None, 'sens', 'grid'), may hold values from 0 to 63
Outputs:
- brightness: float32 [1024, 1024], P(('grid', 'sens'))
The draws below stay inside these ranges and needn't reach their ends.
All inputs are finite; a program needn't handle non-finite values.
Results may differ from the reference program's by a relative error of at most 0.00031.
Values may be sent and summed in bfloat16 or wider, within the bound.
No kernel may reach another device: no remote copies, remote signals or barrier semaphores. Data moves between devices by JAX's collectives and lax.ppermute only.
A program may use at most 64 MiB of HBM per device.

```python
import math
import jax
import jax.numpy as jnp
from jax import lax

NT = 2048
BAND = 128
P_LOW = 160
S_LOW = 48
LAGS = 64
ANCHORS = 1024
SPAN = 1088
SLABS = 8
SENS_SLAB = 128
SENSORS = 1024
NODES = 1024


def draw_records(key, part):
    keys = jax.random.split(key, 3)
    shape = (SLABS, SENS_SLAB, NT)
    row_scale = jnp.exp(jax.random.uniform(keys[1], (SLABS, SENS_SLAB, 1), jnp.float32, 0.0, math.log(10.0)))
    column_scale = jnp.exp(jax.random.uniform(keys[2], (1, 1, NT), jnp.float32, 0.0, math.log(10.0)))
    base = jnp.clip(jax.random.normal(keys[0], shape, jnp.float32), -4.0, 4.0)
    return (base * row_scale * column_scale).astype(jnp.float32)


def place_ends(drawn, own_key, least, high):
    spot = [jax.random.randint(jax.random.fold_in(own_key, axis), (), 0, length) for axis, length in enumerate(drawn.shape)]
    widest = drawn.shape.index(max(drawn.shape))
    neighbour = spot[:widest] + [(spot[widest] + 1) % drawn.shape[widest]] + spot[widest + 1:]
    return drawn.at[tuple(spot)].set(least).at[tuple(neighbour)].set(high)


def setup_inputs(seed: int = 0) -> dict:
    streams_of = jax.random.split(jax.random.key(seed), 4)
    records = draw_records(jax.random.fold_in(streams_of[3], 71), 0)
    travel_p = place_ends(jax.random.randint(streams_of[1], (SLABS, SENS_SLAB, NODES), 0, LAGS), jax.random.fold_in(streams_of[1], 1), 0, LAGS - 1).astype(jnp.int32)
    travel_s = place_ends(jax.random.randint(streams_of[2], (SLABS, SENS_SLAB, NODES), 0, LAGS), jax.random.fold_in(streams_of[2], 1), 0, LAGS - 1).astype(jnp.int32)
    return dict(records=records, travel_p=travel_p, travel_s=travel_s)


def filter_tables():
    samples = jnp.arange(NT, dtype=jnp.int32)
    frequency = jnp.concatenate([jnp.arange(BAND, dtype=jnp.int32) + P_LOW, jnp.arange(BAND, dtype=jnp.int32) + S_LOW])
    angles = (samples[:, None] * frequency[None, :] % NT).astype(jnp.float32) * (2.0 * math.pi / NT)
    forward = jnp.concatenate([jnp.cos(angles), jnp.sin(angles)], axis=1)
    window_samples = jnp.arange(SPAN, dtype=jnp.int32)
    back_angles = (frequency[:, None] * window_samples[None, :] % NT).astype(jnp.float32) * (2.0 * math.pi / NT)
    return (forward, jnp.cos(back_angles), jnp.sin(back_angles))

def characteristic(signals):
    forward, back_cos, back_sin = filter_tables()
    spectrum = jnp.dot(signals, forward, precision=lax.Precision.HIGHEST, preferred_element_type=jnp.float32)
    bands = []
    for band in range(2):
        cos_part = spectrum[:, band * BAND:(band + 1) * BAND]
        sin_part = spectrum[:, (2 + band) * BAND:(3 + band) * BAND]
        coefficients = jnp.concatenate([cos_part, sin_part], axis=1)
        band_cos = back_cos[band * BAND:(band + 1) * BAND]
        band_sin = back_sin[band * BAND:(band + 1) * BAND]
        inverse = jnp.concatenate([jnp.concatenate([band_cos, band_sin], axis=1), jnp.concatenate([band_sin, -band_cos], axis=1)], axis=0) * (2.0 / NT)
        analytic = jnp.dot(coefficients, inverse, precision=lax.Precision.HIGHEST, preferred_element_type=jnp.float32)
        real_part = analytic[:, :SPAN]
        imag_part = analytic[:, SPAN:]
        envelope = jnp.sqrt(real_part * real_part + imag_part * imag_part + 1e-06)
        bands.append(envelope / lax.optimization_barrier(jnp.mean(envelope, axis=1, keepdims=True)) - 1.0)
    return jnp.stack(bands, axis=1).astype(jnp.bfloat16)

def reference(records, travel_p, travel_s):
    signals = records.reshape(-1, NT)
    functions = characteristic(signals).astype(jnp.float32)
    rows_p = travel_p.reshape(-1, NODES)
    rows_s = travel_s.reshape(-1, NODES)
    anchor_offsets = jnp.arange(ANCHORS, dtype=jnp.int32)
    block_size = 8
    count = functions.shape[0] // block_size

    def sensor_values(sensor_cf, shift_p, shift_s):
        first = sensor_cf[0][shift_p[:, None] + anchor_offsets[None, :]]
        second = sensor_cf[1][shift_s[:, None] + anchor_offsets[None, :]]
        return first + second

    def accumulate(total, inputs):
        block_cf, block_p, block_s = inputs
        values = jax.vmap(sensor_values)(block_cf, block_p, block_s)
        return (total + lax.optimization_barrier(jnp.sum(values, axis=0)), None)
    inputs = (functions.reshape(count, block_size, 2, SPAN), rows_p.reshape(count, block_size, NODES), rows_s.reshape(count, block_size, NODES))
    total, unused = lax.scan(accumulate, jnp.zeros((NODES, ANCHORS), jnp.float32), inputs)
    return total * (1.0 / math.sqrt(2.0 * SENSORS))
```

```python
import functools
import math

import jax
import jax.numpy as jnp
import ml_dtypes
import numpy as np
from jax import lax
from jax.experimental import pallas as pl
from jax.experimental.pallas import tpu as pltpu
from jax.sharding import PartitionSpec as P

NT = 2048
HALF = NT // 2
BAND = 128
P_LOW = 160
S_LOW = 48
LAGS = 64
ANCHORS = 1024
SPAN = 1088
FINE = 16
COARSE = LAGS // FINE
ROWS = ANCHORS + FINE
CHUNKS = 4
CHUNK = SPAN // CHUNKS


def split_bf16(table, count):
    pieces = []
    rest = table.astype(np.float32)
    for _ in range(count):
        piece = rest.astype(ml_dtypes.bfloat16)
        pieces.append(piece)
        rest = rest - piece.astype(np.float32)
    return pieces


def bin_order():
    return [(low, parity) for low in (P_LOW, S_LOW) for parity in (0, 1)]


def forward_table():
    samples = np.arange(HALF)
    groups = {0: [], 1: []}
    for low, parity in bin_order():
        bins = low + np.arange(parity, BAND, 2)
        angles = 2.0 * np.pi * ((samples[:, None] * bins[None, :]) % NT) / NT
        groups[parity] += [np.cos(angles), np.sin(angles)]
    table = np.concatenate([np.concatenate(groups[parity], 1) for parity in (0, 1)], 0)
    return np.stack(split_bf16(table, 3))


def inverse_table():
    bins = np.concatenate([np.arange(0, BAND, 2), np.arange(1, BAND, 2)])
    times = np.arange(SPAN)
    angles = 2.0 * np.pi * ((times[:, None] * bins[None, :]) % NT) / NT
    cos, sin = np.cos(angles), np.sin(angles)
    half = BAND // 2
    real = np.concatenate([cos[:, :half], sin[:, :half], cos[:, half:], sin[:, half:]], 1)
    imag = np.concatenate([sin[:, :half], -cos[:, :half], sin[:, half:], -cos[:, half:]], 1)
    both = np.stack([real.reshape(CHUNKS, CHUNK, -1), imag.reshape(CHUNKS, CHUNK, -1)], 1)
    table = both.reshape(2 * SPAN, -1) * (2.0 / NT)
    return np.concatenate(split_bf16(table, 2), 1)


def split_value(value, count):
    pieces = []
    for _ in range(count):
        piece = value.astype(jnp.bfloat16)
        pieces.append(piece)
        value = value - piece.astype(jnp.float32)
    return pieces


def dot(a, b, contract=((1,), (0,))):
    return lax.dot_general(a, b, (contract, ((), ())), preferred_element_type=jnp.float32)


def forward_kernel(records_ref, table_ref, out_ref):
    sensors = records_ref.shape[0]
    early, late = records_ref[:, :HALF], records_ref[:, HALF:]
    for parity, folded in ((0, early + late), (1, early - late)):
        pieces = split_value(folded, 3)
        total = None
        for index in (2, 1, 0):
            stacked = jnp.concatenate(pieces[: 3 - index], axis=0)
            table = table_ref[index, parity * HALF : (parity + 1) * HALF, :]
            product = dot(stacked, table)
            for part in reversed(range(3 - index)):
                term = product[part * sensors : (part + 1) * sensors]
                total = term if total is None else total + term
        for band in range(2):
            column = (2 * band + parity) * BAND
            out_ref[:, column : column + BAND] = total[:, band * BAND : (band + 1) * BAND]


def stack_kernel(axis, spectrum_ref, table_ref, shift_p_ref, shift_s_ref, out_ref,
                 envelope_ref, lagged_ref, hot_ref, sums_ref):
    groups, block = shift_p_ref.shape[0], shift_p_ref.shape[1]
    nodes = shift_p_ref.shape[2]
    count = 2 * groups * block
    spectrum = spectrum_ref[...]
    spectrum = jnp.concatenate([spectrum[:, : 2 * BAND], spectrum[:, 2 * BAND :]], axis=0)
    high, low = split_value(spectrum, 2)
    weights = jnp.concatenate([high, low, high], axis=1)
    mean = jnp.zeros((1, count), jnp.float32)
    for chunk in range(CHUNKS):
        table = table_ref[2 * chunk * CHUNK : 2 * (chunk + 1) * CHUNK, :]
        left = jnp.concatenate([table[:, : 2 * BAND], table], axis=1)
        analytic = dot(left, weights, ((1,), (1,)))
        real, imag = analytic[:CHUNK], analytic[CHUNK:]
        envelope = jnp.sqrt(real * real + imag * imag + 1e-06)
        envelope_ref[chunk * CHUNK : (chunk + 1) * CHUNK, :] = envelope
        mean = mean + jnp.sum(envelope, axis=0, keepdims=True)
    scale = 1.0 / (mean * (1.0 / SPAN))
    for coarse in range(COARSE):
        part = envelope_ref[coarse * FINE : coarse * FINE + ROWS, :] * scale - 1.0
        lagged_ref[:, coarse * count : (coarse + 1) * count] = part.astype(jnp.bfloat16)
    me = lax.axis_index(axis)
    shifts = [ref[me ^ group] for ref in (shift_p_ref, shift_s_ref) for group in range(groups)]
    shifts = jnp.concatenate(shifts, axis=0).astype(jnp.float32).astype(jnp.bfloat16)
    one = jnp.ones((), jnp.bfloat16)
    zero = jnp.zeros((), jnp.bfloat16)
    total = None
    for pair in range(FINE // 2):
        for coarse in range(COARSE):
            for side in range(2):
                lag = coarse * FINE + 2 * pair + side
                hot_ref[coarse * count : (coarse + 1) * count, side * nodes : (side + 1) * nodes] = (
                    jnp.where(shifts == jnp.bfloat16(lag), one, zero)
                )
        sums_ref[...] = dot(lagged_ref[...], hot_ref[...])
        for side in range(2):
            fine = 2 * pair + side
            term = sums_ref[fine : fine + ANCHORS, side * nodes : (side + 1) * nodes]
            total = term if total is None else total + term
    out_ref[...] = total.T


def gather_spectra(spectrum, axis):
    size = lax.axis_size(axis)

    def exchange(value, offset):
        return lax.ppermute(value, axis, [(i, i ^ offset) for i in range(size)])

    blocks = [spectrum] + [exchange(spectrum, offset) for offset in range(1, size)]
    return jnp.concatenate(blocks, axis=0)


def scatter_sum(stacked, axis):
    size = lax.axis_size(axis)
    here = lax.axis_index(axis)
    parts = stacked.reshape(size, stacked.shape[0] // size, stacked.shape[1])
    total = lax.dynamic_index_in_dim(parts, here, 0, False)
    for offset in reversed(range(1, size)):
        part = lax.dynamic_index_in_dim(parts, (here + offset) % size, 0, False)
        total = total + lax.ppermute(part, axis, [(i, (i + offset) % size) for i in range(size)])
    return total


def per_device(records, travel_p, travel_s):
    groups, sensors, nodes = travel_p.shape
    count = 2 * groups * sensors
    spectrum = pl.pallas_call(
        forward_kernel,
        out_shape=jax.ShapeDtypeStruct((sensors, 4 * BAND), jnp.float32),
        compiler_params=pltpu.CompilerParams(vmem_limit_bytes=32 << 20),
    )(records[0], jnp.asarray(forward_table()))
    spectra = gather_spectra(spectrum, "grid")
    stacked = pl.pallas_call(
        functools.partial(stack_kernel, "grid"),
        out_shape=jax.ShapeDtypeStruct((nodes, ANCHORS), jnp.float32),
        scratch_shapes=[
            pltpu.VMEM((SPAN, count), jnp.float32),
            pltpu.VMEM((ROWS, COARSE * count), jnp.bfloat16),
            pltpu.VMEM((COARSE * count, 2 * nodes), jnp.bfloat16),
            pltpu.VMEM((ROWS, 2 * nodes), jnp.float32),
        ],
        compiler_params=pltpu.CompilerParams(vmem_limit_bytes=56 << 20),
    )(spectra, jnp.asarray(inverse_table()), travel_p, travel_s)
    sensor_total = sensors * lax.axis_size("grid") * lax.axis_size("sens")
    return scatter_sum(stacked, "sens") * (1.0 / math.sqrt(2.0 * sensor_total))


def solution(mesh):
    return jax.shard_map(
        per_device,
        mesh=mesh,
        in_specs=(P("grid", "sens", None), P(None, "sens", "grid"), P(None, "sens", "grid")),
        out_specs=P(("grid", "sens"), None),
        check_vma=False,
    )
```

```python
import functools
import math

import jax
import jax.numpy as jnp
import ml_dtypes
import numpy as np
from jax import lax
from jax.experimental import pallas as pl
from jax.experimental.pallas import tpu as pltpu
from jax.sharding import PartitionSpec as P

NT = 2048
HALF = NT // 2
BAND = 128
P_LOW = 160
S_LOW = 48
LAGS = 64
ANCHORS = 1024
SPAN = 1088
FINE = 16
COARSE = LAGS // FINE
ROWS = ANCHORS + FINE
CHUNKS = 4
CHUNK = SPAN // CHUNKS


def split_bf16(table, count):
    pieces = []
    rest = table.astype(np.float32)
    for _ in range(count):
        piece = rest.astype(ml_dtypes.bfloat16)
        pieces.append(piece)
        rest = rest - piece.astype(np.float32)
    return pieces


def bin_order():
    return [(low, parity) for low in (P_LOW, S_LOW) for parity in (0, 1)]


def forward_table():
    samples = np.arange(HALF)
    groups = {0: [], 1: []}
    for low, parity in bin_order():
        bins = low + np.arange(parity, BAND, 2)
        angles = 2.0 * np.pi * ((samples[:, None] * bins[None, :]) % NT) / NT
        groups[parity] += [np.cos(angles), np.sin(angles)]
    return np.stack([np.stack(split_bf16(np.concatenate(groups[p], 1), 3)) for p in (0, 1)])


def inverse_table():
    bins = np.concatenate([np.arange(0, BAND, 2), np.arange(1, BAND, 2)])
    times = np.arange(SPAN)
    angles = 2.0 * np.pi * ((times[:, None] * bins[None, :]) % NT) / NT
    cos, sin = np.cos(angles), np.sin(angles)
    half = BAND // 2
    real = np.concatenate([cos[:, :half], sin[:, :half], cos[:, half:], sin[:, half:]], 1)
    imag = np.concatenate([sin[:, :half], -cos[:, :half], sin[:, half:], -cos[:, half:]], 1)
    both = np.stack([real.reshape(CHUNKS, CHUNK, -1), imag.reshape(CHUNKS, CHUNK, -1)], 1)
    table = both.reshape(2 * SPAN, -1) * (2.0 / NT)
    return np.concatenate(split_bf16(table, 2), 1)


def split_value(value, count):
    pieces = []
    for _ in range(count):
        piece = value.astype(jnp.bfloat16)
        pieces.append(piece)
        value = value - piece.astype(jnp.float32)
    return pieces


def dot(a, b, contract=((1,), (0,))):
    return lax.dot_general(a, b, (contract, ((), ())), preferred_element_type=jnp.float32)


def forward_kernel(records_hbm, table_hbm, out_ref, records_ref, table_ref, sems):
    copies = [
        pltpu.make_async_copy(records_hbm, records_ref, sems.at[0]),
        pltpu.make_async_copy(table_hbm.at[0], table_ref.at[0], sems.at[1]),
        pltpu.make_async_copy(table_hbm.at[1], table_ref.at[1], sems.at[2]),
    ]
    for copy in copies:
        copy.start()
    copies[0].wait()
    sensors = records_ref.shape[0]
    early, late = records_ref[:, :HALF], records_ref[:, HALF:]
    for parity, folded in ((0, early + late), (1, early - late)):
        pieces = split_value(folded, 3)
        copies[1 + parity].wait()
        total = None
        for index in (2, 1, 0):
            stacked = jnp.concatenate(pieces[: 3 - index], axis=0)
            product = dot(stacked, table_ref[parity, index])
            for part in reversed(range(3 - index)):
                term = product[part * sensors : (part + 1) * sensors]
                total = term if total is None else total + term
        for band in range(2):
            column = (2 * band + parity) * BAND
            out_ref[:, column : column + BAND] = total[:, band * BAND : (band + 1) * BAND]


def group_order(size, here):
    if size != 8:
        return [here ^ offset for offset in range(size)]
    first = 2 + 2 * (here & 1)
    second = 6 - first
    own = [here, here ^ first, here ^ second, here ^ 6]
    other = here ^ 1
    return own + [other, other ^ second, other ^ first, other ^ 6]


def shift_kernel(axis, owner_axis, shift_p_ref, shift_s_ref, out_ref, turned_ref):
    groups, block, nodes = shift_p_ref.shape
    parts = out_ref.shape[0]
    width = nodes // parts
    order = group_order(groups, lax.axis_index(axis))
    rows = [ref[group] for ref in (shift_p_ref, shift_s_ref) for group in order]
    shifts = jnp.concatenate(rows, axis=0).astype(jnp.float32)
    lane = lax.broadcasted_iota(jnp.int32, shifts.shape, 1) // width
    for turn in range(parts):
        turned_ref[turn] = pltpu.roll(shifts, turn * width, 1) if turn else shifts
    owner = lax.axis_index(owner_axis)
    for offset in range(parts):
        target = owner ^ offset
        spread = turned_ref[(parts - target) & (parts - 1)]
        for place in range(1, parts):
            turned = turned_ref[(place - target) & (parts - 1)]
            spread = jnp.where(lane == place, turned, spread)
        out_ref[offset] = (spread - lane.astype(jnp.float32)).astype(jnp.bfloat16)


def function_kernel(*refs):
    spectrum_refs, (table_ref, out_ref, envelope_ref) = refs[:-3], refs[-3:]
    count = out_ref.shape[1]
    spectrum = jnp.concatenate([ref[...] for ref in spectrum_refs], axis=0)
    spectrum = jnp.concatenate([spectrum[:, : 2 * BAND], spectrum[:, 2 * BAND :]], axis=0)
    high, low = split_value(spectrum, 2)
    weights = jnp.concatenate([high, low, high], axis=1)
    total = jnp.zeros((1, count), jnp.float32)
    for chunk in range(CHUNKS):
        table = table_ref[2 * chunk * CHUNK : 2 * (chunk + 1) * CHUNK, :]
        left = jnp.concatenate([table[:, : 2 * BAND], table], axis=1)
        analytic = dot(left, weights, ((1,), (1,)))
        real, imag = analytic[:CHUNK], analytic[CHUNK:]
        envelope = jnp.sqrt(real * real + imag * imag + 1e-06)
        envelope_ref[chunk * CHUNK : (chunk + 1) * CHUNK, :] = envelope
        total = total + jnp.sum(envelope, axis=0, keepdims=True)
    scale = 1.0 / (total * (1.0 / SPAN))
    out_ref[...] = (envelope_ref[...] * scale - 1.0).astype(jnp.bfloat16)


def stack_kernel(offset, functions_ref, shifts_ref, out_ref, hot_ref, sums_ref, near_ref):
    parts, count, nodes = shifts_ref.shape
    blocks = FINE // parts
    width = nodes // parts
    shifts = shifts_ref[offset]
    one = jnp.ones((), jnp.bfloat16)
    zero = jnp.zeros((), jnp.bfloat16)
    for coarse in range(COARSE):
        for block in range(blocks):
            lag = jnp.bfloat16(coarse * FINE + block * parts)
            hot_ref[coarse * count : (coarse + 1) * count, block * nodes : (block + 1) * nodes] = (
                jnp.where(shifts == lag, one, zero)
            )
    lagged = [functions_ref[c * FINE : c * FINE + ROWS, :] for c in range(COARSE)]
    sums_ref[...] = dot(jnp.concatenate(lagged, axis=1), hot_ref[...])
    for first, rows in ((0, ANCHORS), (ANCHORS, parts)):
        near = None
        for block in range(blocks):
            row = first + block * parts
            term = sums_ref[row : row + rows, block * nodes : (block + 1) * nodes]
            near = term if near is None else near + term
        near_ref[first : first + rows, :] = near
    lane = lax.broadcasted_iota(jnp.int32, (ANCHORS, nodes), 1) // width
    total = near_ref[:ANCHORS, :]
    for place in range(1, parts):
        total = jnp.where(lane == place, near_ref[place : place + ANCHORS, :], total)
    turned = total.T
    result = turned[:width]
    for place in range(1, parts):
        result = result + turned[place * width : (place + 1) * width]
    out_ref[...] = result


def exchange(value, axis, offset):
    size = lax.axis_size(axis)
    return lax.ppermute(value, axis, [(i, i ^ offset) for i in range(size)])


def gather_spectra(spectrum, axis):
    size = lax.axis_size(axis)
    if size != 8:
        return [spectrum] + [exchange(spectrum, axis, offset) for offset in range(1, size)]
    first = lax.ppermute(spectrum, axis, [(i, i ^ (2 + 2 * (i & 1))) for i in range(size)])
    second = lax.ppermute(spectrum, axis, [(i, i ^ (4 - 2 * (i & 1))) for i in range(size)])
    third = exchange(spectrum, axis, 6)
    own = exchange(spectrum, axis, 1)
    others = jnp.concatenate([first, second, third], axis=0)
    return [spectrum, others, own, exchange(others, axis, 1)]


def per_device(records, travel_p, travel_s):
    groups, sensors, nodes = travel_p.shape
    count = 2 * groups * sensors
    parts = lax.axis_size("sens")
    width = nodes // parts
    table = forward_table()
    spectrum = pl.pallas_call(
        forward_kernel,
        out_shape=jax.ShapeDtypeStruct((sensors, 4 * BAND), jnp.float32),
        in_specs=[pl.BlockSpec(memory_space=pltpu.HBM)] * 2,
        scratch_shapes=[
            pltpu.VMEM((sensors, NT), jnp.float32),
            pltpu.VMEM(table.shape, jnp.bfloat16),
            pltpu.SemaphoreType.DMA((3,)),
        ],
        compiler_params=pltpu.CompilerParams(vmem_limit_bytes=16 << 20),
    )(records[0], jnp.asarray(table))
    shifts = pl.pallas_call(
        functools.partial(shift_kernel, "grid", "sens"),
        out_shape=jax.ShapeDtypeStruct((parts, count, nodes), jnp.bfloat16),
        scratch_shapes=[pltpu.VMEM((parts, count, nodes), jnp.float32)],
        compiler_params=pltpu.CompilerParams(vmem_limit_bytes=16 << 20),
        cost_estimate=pl.CostEstimate(
            flops=parts * parts * count * nodes, bytes_accessed=4 * count * nodes, transcendentals=0
        ),
    )(travel_p, travel_s)
    functions = pl.pallas_call(
        function_kernel,
        out_shape=jax.ShapeDtypeStruct((SPAN, count), jnp.bfloat16),
        scratch_shapes=[pltpu.VMEM((SPAN, count), jnp.float32)],
        compiler_params=pltpu.CompilerParams(vmem_limit_bytes=28 << 20),
    )(*gather_spectra(spectrum, "grid"), jnp.asarray(inverse_table()))

    def stack(offset):
        return pl.pallas_call(
            functools.partial(stack_kernel, offset),
            out_shape=jax.ShapeDtypeStruct((width, ANCHORS), jnp.float32),
            scratch_shapes=[
                pltpu.VMEM((COARSE * count, FINE // parts * nodes), jnp.bfloat16),
                pltpu.VMEM((ROWS, FINE // parts * nodes), jnp.float32),
                pltpu.VMEM((ANCHORS + 8, nodes), jnp.float32),
            ],
            compiler_params=pltpu.CompilerParams(vmem_limit_bytes=28 << 20),
            cost_estimate=pl.CostEstimate(
                flops=2 * ROWS * COARSE * count * (FINE // parts) * nodes,
                bytes_accessed=2 * SPAN * count,
                transcendentals=0,
            ),
        )(functions, shifts)

    if parts == 4:
        passing = exchange(stack(3), "sens", 1)
        crossing = exchange(stack(2) + passing, "sens", 2)
        nearby = exchange(stack(1), "sens", 1)
        total = stack(0) + crossing + nearby
    else:
        arrived = [exchange(stack(offset), "sens", offset) for offset in reversed(range(1, parts))]
        total = stack(0)
        for part in arrived:
            total = total + part
    sensor_total = sensors * lax.axis_size("grid") * parts
    return total * (1.0 / math.sqrt(2.0 * sensor_total))


def solution(mesh):
    return jax.shard_map(
        per_device,
        mesh=mesh,
        in_specs=(P("grid", "sens", None), P(None, "sens", "grid"), P(None, "sens", "grid")),
        out_specs=P(("grid", "sens"), None),
        check_vma=False,
    )
```

```python
import functools
import math

import jax
import jax.numpy as jnp
import ml_dtypes
import numpy as np
from jax import lax
from jax.experimental import pallas as pl
from jax.experimental.pallas import tpu as pltpu
from jax.sharding import PartitionSpec as P

NT = 2048
HALF = NT // 2
BAND = 128
P_LOW = 160
S_LOW = 48
LAGS = 64
ANCHORS = 1024
SPAN = 1088
FINE = 16
COARSE = LAGS // FINE
ROWS = ANCHORS + FINE
STEP = 32
CHUNKS = 4
CHUNK = SPAN // CHUNKS


def split_bf16(table, count):
    pieces = []
    rest = table.astype(np.float32)
    for _ in range(count):
        piece = rest.astype(ml_dtypes.bfloat16)
        pieces.append(piece)
        rest = rest - piece.astype(np.float32)
    return pieces


def inverse_table():
    times = np.arange(SPAN)
    columns = []
    for parity in (0, 1):
        bins = np.arange(parity, BAND, 2)
        angles = 2.0 * np.pi * ((times[:, None] * bins[None, :]) % NT) / NT
        columns += [np.cos(angles), np.sin(angles)]
    return np.concatenate(split_bf16(np.concatenate(columns, 1) * (2.0 / NT), 2), 1)


def split_value(value, count):
    pieces = []
    for _ in range(count):
        piece = value.astype(jnp.bfloat16)
        pieces.append(piece)
        value = value - piece.astype(jnp.float32)
    return pieces


def dot(a, b, contract=((1,), (0,))):
    return lax.dot_general(a, b, (contract, ((), ())), preferred_element_type=jnp.float32)


def group_order(size, here):
    if size != 8:
        return [here ^ offset for offset in range(size)]
    first = 2 + 2 * (here & 1)
    second = 6 - first
    own = [here, here ^ first, here ^ second, here ^ 6]
    other = here ^ 1
    return own + [other, other ^ second, other ^ first, other ^ 6]


def shift_kernel(axis, owner_axis, shift_p_ref, shift_s_ref, out_ref, turned_ref):
    groups, block, nodes = shift_p_ref.shape
    parts = out_ref.shape[0]
    width = nodes // parts
    order = group_order(groups, lax.axis_index(axis))
    rows = [ref[group] for ref in (shift_p_ref, shift_s_ref) for group in order]
    shifts = jnp.concatenate(rows, axis=0).astype(jnp.float32)
    lane = lax.broadcasted_iota(jnp.int32, shifts.shape, 1) // width
    for turn in range(parts):
        turned_ref[turn] = pltpu.roll(shifts, turn * width, 1) if turn else shifts
    owner = lax.axis_index(owner_axis)
    for offset in range(parts):
        target = owner ^ offset
        spread = turned_ref[(parts - target) & (parts - 1)]
        for place in range(1, parts):
            turned = turned_ref[(place - target) & (parts - 1)]
            spread = jnp.where(lane == place, turned, spread)
        out_ref[offset] = (spread - lane.astype(jnp.float32)).astype(jnp.bfloat16)


def table_kernel(table_ref):
    half = BAND // 2
    lane = lax.broadcasted_iota(jnp.int32, (STEP, BAND), 1)
    row = lax.broadcasted_iota(jnp.int32, (STEP, BAND), 0)
    bins = jnp.where(lane < half, P_LOW + 2 * lane, S_LOW + 2 * (lane - half))
    for parity in (0, 1):
        fine = ((row * (bins + parity)) & (NT - 1)).astype(jnp.float32) * (2.0 * math.pi / NT)
        base = ((row * STEP * (bins + parity)) & (NT - 1)).astype(jnp.float32) * (2.0 * math.pi / NT)
        fine_cos, fine_sin = jnp.cos(fine), jnp.sin(fine)
        base_cos, base_sin = jnp.cos(base), jnp.sin(base)
        for step in range(HALF // STEP):
            step_cos, step_sin = base_cos[step : step + 1], base_sin[step : step + 1]
            rows = slice(step * STEP, (step + 1) * STEP)
            for column, value in (
                (0, step_cos * fine_cos - step_sin * fine_sin),
                (BAND, step_sin * fine_cos + step_cos * fine_sin),
            ):
                for index, piece in enumerate(split_value(value, 3)):
                    table_ref[parity, index, rows, column : column + BAND] = piece


def forward_kernel(records_ref, table_ref, out_ref):
    sensors = records_ref.shape[0]
    half = BAND // 2
    early, late = records_ref[:, :HALF], records_ref[:, HALF:]
    for parity, folded in ((0, early + late), (1, early - late)):
        pieces = split_value(folded, 3)
        total = None
        for index in (2, 1, 0):
            stacked = jnp.concatenate(pieces[: 3 - index], axis=0)
            product = dot(stacked, table_ref[parity, index])
            for part in reversed(range(3 - index)):
                term = product[part * sensors : (part + 1) * sensors]
                total = term if total is None else total + term
        for band in range(2):
            column = (2 * band + parity) * BAND
            for side in range(2):
                first = side * BAND + band * half
                out_ref[:, column + side * half : column + (side + 1) * half] = total[:, first : first + half]


def function_kernel(*refs):
    spectrum_refs, (table_ref, out_ref, envelope_ref) = refs[:-3], refs[-3:]
    count = out_ref.shape[1]
    spectrum = jnp.concatenate([ref[...] for ref in spectrum_refs], axis=0)
    spectrum = jnp.concatenate([spectrum[:, : 2 * BAND], spectrum[:, 2 * BAND :]], axis=0)
    half = BAND // 2
    blocks = []
    for first in (0, BAND):
        block = pltpu.roll(spectrum[:, first : first + BAND], half, 1)
        lane = lax.broadcasted_iota(jnp.int32, block.shape, 1)
        blocks.append(jnp.where(lane < half, -block, block))
    spectrum = jnp.concatenate([spectrum, jnp.concatenate(blocks, axis=1)], axis=0)
    high, low = split_value(spectrum, 2)
    weights = jnp.concatenate([high, low, high], axis=1)
    total = jnp.zeros((1, count), jnp.float32)
    for chunk in range(CHUNKS):
        table = table_ref[chunk * CHUNK : (chunk + 1) * CHUNK, :]
        left = jnp.concatenate([table[:, : 2 * BAND], table], axis=1)
        analytic = dot(left, weights, ((1,), (1,)))
        real, imag = analytic[:, :count], analytic[:, count:]
        envelope = jnp.sqrt(real * real + imag * imag + 1e-06)
        envelope_ref[chunk * CHUNK : (chunk + 1) * CHUNK, :] = envelope
        total = total + jnp.sum(envelope, axis=0, keepdims=True)
    scale = 1.0 / (total * (1.0 / SPAN))
    out_ref[...] = (envelope_ref[...] * scale - 1.0).astype(jnp.bfloat16)


def stack_kernel(offset, functions_ref, shifts_ref, out_ref, hot_ref, sums_ref, near_ref):
    parts, count, nodes = shifts_ref.shape
    blocks = FINE // parts
    width = nodes // parts
    shifts = shifts_ref[offset]
    one = jnp.ones((), jnp.bfloat16)
    zero = jnp.zeros((), jnp.bfloat16)
    for coarse in range(COARSE):
        for block in range(blocks):
            lag = jnp.bfloat16(coarse * FINE + block * parts)
            hot_ref[coarse * count : (coarse + 1) * count, block * nodes : (block + 1) * nodes] = (
                jnp.where(shifts == lag, one, zero)
            )
    lagged = [functions_ref[c * FINE : c * FINE + ROWS, :] for c in range(COARSE)]
    sums_ref[...] = dot(jnp.concatenate(lagged, axis=1), hot_ref[...])
    for first, rows in ((0, ANCHORS), (ANCHORS, parts)):
        near = None
        for block in range(blocks):
            row = first + block * parts
            term = sums_ref[row : row + rows, block * nodes : (block + 1) * nodes]
            near = term if near is None else near + term
        near_ref[first : first + rows, :] = near
    lane = lax.broadcasted_iota(jnp.int32, (ANCHORS, nodes), 1) // width
    total = near_ref[:ANCHORS, :]
    for place in range(1, parts):
        total = jnp.where(lane == place, near_ref[place : place + ANCHORS, :], total)
    turned = total.T
    result = turned[:width]
    for place in range(1, parts):
        result = result + turned[place * width : (place + 1) * width]
    out_ref[...] = result


def exchange(value, axis, offset):
    size = lax.axis_size(axis)
    return lax.ppermute(value, axis, [(i, i ^ offset) for i in range(size)])


def gather_spectra(spectrum, axis, beside):
    size = lax.axis_size(axis)
    if size != 8:
        return [spectrum] + [exchange(spectrum, axis, offset) for offset in range(1, size)], beside
    first = lax.ppermute(spectrum, axis, [(i, i ^ (2 + 2 * (i & 1))) for i in range(size)])
    second = lax.ppermute(spectrum, axis, [(i, i ^ (4 - 2 * (i & 1))) for i in range(size)])
    third = exchange(spectrum, axis, 6)
    first, beside = lax.optimization_barrier((first, beside))
    chips = [spectrum, first, second, third]
    return chips + [exchange(chip, axis, 1) for chip in chips], beside


def per_device(records, travel_p, travel_s):
    groups, sensors, nodes = travel_p.shape
    count = 2 * groups * sensors
    parts = lax.axis_size("sens")
    width = nodes // parts
    limit = pltpu.CompilerParams(vmem_limit_bytes=24 << 20)
    table = pl.pallas_call(
        table_kernel,
        out_shape=jax.ShapeDtypeStruct((2, 3, HALF, 2 * BAND), jnp.bfloat16),
        compiler_params=limit,
        cost_estimate=pl.CostEstimate(flops=16 * HALF * 4 * BAND, bytes_accessed=0, transcendentals=0),
    )()
    spectrum = pl.pallas_call(
        forward_kernel,
        out_shape=jax.ShapeDtypeStruct((sensors, 4 * BAND), jnp.float32),
        compiler_params=limit,
    )(records[0], table)
    shifts = pl.pallas_call(
        functools.partial(shift_kernel, "grid", "sens"),
        out_shape=jax.ShapeDtypeStruct((parts, count, nodes), jnp.bfloat16),
        scratch_shapes=[pltpu.VMEM((parts, count, nodes), jnp.float32)],
        compiler_params=limit,
        cost_estimate=pl.CostEstimate(
            flops=parts * parts * count * nodes, bytes_accessed=4 * count * nodes, transcendentals=0
        ),
    )(travel_p, travel_s)
    spectra, shifts = gather_spectra(spectrum, "grid", shifts)
    functions = pl.pallas_call(
        function_kernel,
        out_shape=jax.ShapeDtypeStruct((SPAN, count), jnp.bfloat16),
        scratch_shapes=[pltpu.VMEM((SPAN, count), jnp.float32)],
        compiler_params=pltpu.CompilerParams(vmem_limit_bytes=28 << 20),
    )(*spectra, jnp.asarray(inverse_table()))

    def stack(offset, functions):
        return pl.pallas_call(
            functools.partial(stack_kernel, offset),
            out_shape=jax.ShapeDtypeStruct((width, ANCHORS), jnp.float32),
            scratch_shapes=[
                pltpu.VMEM((COARSE * count, FINE // parts * nodes), jnp.bfloat16),
                pltpu.VMEM((ROWS, FINE // parts * nodes), jnp.float32),
                pltpu.VMEM((ANCHORS + 8, nodes), jnp.float32),
            ],
            compiler_params=pltpu.CompilerParams(vmem_limit_bytes=28 << 20),
            cost_estimate=pl.CostEstimate(flops=1024, bytes_accessed=1024, transcendentals=0),
        )(functions, shifts)

    if parts == 4:
        far = stack(3, functions)
        passing = exchange(far, "sens", 1)
        functions, far = lax.optimization_barrier((functions, far))
        near = stack(1, functions)
        nearby = exchange(near, "sens", 1)
        functions, near = lax.optimization_barrier((functions, near))
        paired = stack(2, functions) + passing
        crossing = exchange(paired, "sens", 2)
        functions, paired = lax.optimization_barrier((functions, paired))
        total = stack(0, functions) + crossing + nearby
    else:
        offsets = reversed(range(1, parts))
        arrived = [exchange(stack(offset, functions), "sens", offset) for offset in offsets]
        total = stack(0, functions)
        for part in arrived:
            total = total + part
    sensor_total = sensors * lax.axis_size("grid") * parts
    return total * (1.0 / math.sqrt(2.0 * sensor_total))


def solution(mesh):
    return jax.shard_map(
        per_device,
        mesh=mesh,
        in_specs=(P("grid", "sens", None), P(None, "sens", "grid"), P(None, "sens", "grid")),
        out_specs=P(("grid", "sens"), None),
        check_vma=False,
    )
```

```python
import functools
import math

import jax
import jax.numpy as jnp
import ml_dtypes
import numpy as np
from jax import lax
from jax.experimental import pallas as pl
from jax.experimental.pallas import tpu as pltpu
from jax.sharding import PartitionSpec as P

NT = 2048
HALF = NT // 2
BAND = 128
P_LOW = 160
S_LOW = 48
LAGS = 64
ANCHORS = 1024
SPAN = 1088
FINE = 16
COARSE = LAGS // FINE
ROWS = ANCHORS + FINE
STEP = 32
LEVELS = 32000.0
CHUNKS = 4
CHUNK = SPAN // CHUNKS


def split_bf16(table, count):
    pieces = []
    rest = table.astype(np.float32)
    for _ in range(count):
        piece = rest.astype(ml_dtypes.bfloat16)
        pieces.append(piece)
        rest = rest - piece.astype(np.float32)
    return pieces


def inverse_table():
    times = np.arange(SPAN)
    columns = []
    for parity in (0, 1):
        bins = np.arange(parity, BAND, 2)
        angles = 2.0 * np.pi * ((times[:, None] * bins[None, :]) % NT) / NT
        columns += [np.cos(angles), np.sin(angles)]
    return np.concatenate(split_bf16(np.concatenate(columns, 1) * (2.0 / NT), 2), 1)


def split_value(value, count):
    pieces = []
    for _ in range(count):
        piece = value.astype(jnp.bfloat16)
        pieces.append(piece)
        value = value - piece.astype(jnp.float32)
    return pieces


def dot(a, b, contract=((1,), (0,))):
    return lax.dot_general(a, b, (contract, ((), ())), preferred_element_type=jnp.float32)


def group_order(size, here):
    if size != 8:
        return [here ^ offset for offset in range(size)]
    near = 2 + 2 * (here & 1)
    far = 6 - near
    mine = [here, here ^ 1, here ^ near, here ^ near ^ 1, here ^ 6]
    return mine + [here ^ 1 ^ far, here ^ far, here ^ 7]


def shift_kernel(axis, owner_axis, shift_p_ref, shift_s_ref, out_ref, turned_ref):
    groups, block, nodes = shift_p_ref.shape
    parts = out_ref.shape[0]
    width = nodes // parts
    order = group_order(groups, lax.axis_index(axis))
    rows = [ref[group] for ref in (shift_p_ref, shift_s_ref) for group in order]
    shifts = jnp.concatenate(rows, axis=0).astype(jnp.float32)
    lane = lax.broadcasted_iota(jnp.int32, shifts.shape, 1) // width
    for turn in range(parts):
        turned_ref[turn] = pltpu.roll(shifts, turn * width, 1) if turn else shifts
    owner = lax.axis_index(owner_axis)
    for offset in range(parts):
        target = owner ^ offset
        spread = turned_ref[(parts - target) & (parts - 1)]
        for place in range(1, parts):
            turned = turned_ref[(place - target) & (parts - 1)]
            spread = jnp.where(lane == place, turned, spread)
        out_ref[offset] = (spread - lane.astype(jnp.float32)).astype(jnp.bfloat16)


def table_kernel(table_ref):
    half = BAND // 2
    lane = lax.broadcasted_iota(jnp.int32, (STEP, BAND), 1)
    row = lax.broadcasted_iota(jnp.int32, (STEP, BAND), 0)
    bins = jnp.where(lane < half, P_LOW + 2 * lane, S_LOW + 2 * (lane - half))
    for parity in (0, 1):
        fine = ((row * (bins + parity)) & (NT - 1)).astype(jnp.float32) * (2.0 * math.pi / NT)
        base = ((row * STEP * (bins + parity)) & (NT - 1)).astype(jnp.float32) * (2.0 * math.pi / NT)
        fine_cos, fine_sin = jnp.cos(fine), jnp.sin(fine)
        base_cos, base_sin = jnp.cos(base), jnp.sin(base)
        for step in range(HALF // STEP):
            step_cos, step_sin = base_cos[step : step + 1], base_sin[step : step + 1]
            rows = slice(step * STEP, (step + 1) * STEP)
            for column, value in (
                (0, step_cos * fine_cos - step_sin * fine_sin),
                (BAND, step_sin * fine_cos + step_cos * fine_sin),
            ):
                for index, piece in enumerate(split_value(value, 3)):
                    table_ref[parity, index, rows, column : column + BAND] = piece


def forward_kernel(records_ref, table_ref, out_ref):
    sensors = records_ref.shape[0]
    half = BAND // 2
    early, late = records_ref[:, :HALF], records_ref[:, HALF:]
    for parity, folded in ((0, early + late), (1, early - late)):
        pieces = split_value(folded, 3)
        total = None
        for index in (2, 1, 0):
            stacked = jnp.concatenate(pieces[: 3 - index], axis=0)
            product = dot(stacked, table_ref[parity, index])
            for part in reversed(range(3 - index)):
                term = product[part * sensors : (part + 1) * sensors]
                total = term if total is None else total + term
        for band in range(2):
            column = (2 * band + parity) * BAND
            for side in range(2):
                first = side * BAND + band * half
                out_ref[:, column + side * half : column + (side + 1) * half] = total[:, first : first + half]


def function_kernel(*refs):
    spectrum_refs, (table_ref, out_ref, envelope_ref) = refs[:-3], refs[-3:]
    count = out_ref.shape[1]
    spectrum = jnp.concatenate([ref[...] for ref in spectrum_refs], axis=0)
    spectrum = jnp.concatenate([spectrum[:, : 2 * BAND], spectrum[:, 2 * BAND :]], axis=0)
    half = BAND // 2
    blocks = []
    for first in (0, BAND):
        block = pltpu.roll(spectrum[:, first : first + BAND], half, 1)
        lane = lax.broadcasted_iota(jnp.int32, block.shape, 1)
        blocks.append(jnp.where(lane < half, -block, block))
    spectrum = jnp.concatenate([spectrum, jnp.concatenate(blocks, axis=1)], axis=0)
    high, low = split_value(spectrum, 2)
    weights = jnp.concatenate([high, low, high], axis=1)
    total = jnp.zeros((1, count), jnp.float32)
    for chunk in range(CHUNKS):
        table = table_ref[chunk * CHUNK : (chunk + 1) * CHUNK, :]
        left = jnp.concatenate([table[:, : 2 * BAND], table], axis=1)
        analytic = dot(left, weights, ((1,), (1,)))
        real, imag = analytic[:, :count], analytic[:, count:]
        envelope = jnp.sqrt(real * real + imag * imag + 1e-06)
        envelope_ref[chunk * CHUNK : (chunk + 1) * CHUNK, :] = envelope
        total = total + jnp.sum(envelope, axis=0, keepdims=True)
    scale = 1.0 / (total * (1.0 / SPAN))
    out_ref[...] = (envelope_ref[...] * scale - 1.0).astype(jnp.bfloat16)


def step_size(code):
    return jnp.exp2(code * 0.125) * (1.0 / LEVELS)


def encode(value):
    largest = jnp.max(jnp.abs(value), axis=1, keepdims=True)
    code = jnp.floor(8.0 * jnp.log2(jnp.maximum(largest, 1e-30))) + 1.0
    levels = jnp.round(value * (1.0 / step_size(code))).astype(jnp.int32)
    codes = jnp.broadcast_to(code, (value.shape[0], 128)).astype(jnp.int32)
    return jnp.concatenate([levels, codes], axis=1).astype(jnp.int16)


def decode(coded):
    columns = coded.shape[1] - 128
    code = coded[:, columns : columns + 1].astype(jnp.float32)
    return coded[:, :columns].astype(jnp.float32) * step_size(code)


def stack_kernel(offset, functions_ref, shifts_ref, *refs):
    extra_refs, (out_ref, hot_ref, sums_ref, near_ref) = refs[:-4], refs[-4:]
    parts, count, nodes = shifts_ref.shape
    blocks = FINE // parts
    width = nodes // parts
    shifts = shifts_ref[offset]
    one = jnp.ones((), jnp.bfloat16)
    zero = jnp.zeros((), jnp.bfloat16)
    for coarse in range(COARSE):
        for block in range(blocks):
            lag = jnp.bfloat16(coarse * FINE + block * parts)
            hot_ref[coarse * count : (coarse + 1) * count, block * nodes : (block + 1) * nodes] = (
                jnp.where(shifts == lag, one, zero)
            )
    lagged = [functions_ref[c * FINE : c * FINE + ROWS, :] for c in range(COARSE)]
    sums_ref[...] = dot(jnp.concatenate(lagged, axis=1), hot_ref[...])
    for first, rows in ((0, ANCHORS), (ANCHORS, parts)):
        near = None
        for block in range(blocks):
            row = first + block * parts
            term = sums_ref[row : row + rows, block * nodes : (block + 1) * nodes]
            near = term if near is None else near + term
        near_ref[first : first + rows, :] = near
    lane = lax.broadcasted_iota(jnp.int32, (ANCHORS, nodes), 1) // width
    total = near_ref[:ANCHORS, :]
    for place in range(1, parts):
        total = jnp.where(lane == place, near_ref[place : place + ANCHORS, :], total)
    turned = total.T
    result = turned[:width]
    for place in range(1, parts):
        result = result + turned[place * width : (place + 1) * width]
    for ref in extra_refs:
        result = result + decode(ref[...])
    out_ref[...] = encode(result) if out_ref.dtype == jnp.int16 else result


def exchange(value, axis, offset):
    size = lax.axis_size(axis)
    return lax.ppermute(value, axis, [(i, i ^ offset) for i in range(size)])


def gather_spectra(spectrum, axis, beside):
    size = lax.axis_size(axis)
    if size != 8:
        return [spectrum] + [exchange(spectrum, axis, offset) for offset in range(1, size)], beside
    partners = [(i, i ^ (2 + 2 * (i & 1))) for i in range(size)]
    sibling = exchange(spectrum, axis, 1)
    diagonal = exchange(spectrum, axis, 6)
    first = lax.ppermute(spectrum, axis, partners)
    second = lax.ppermute(sibling, axis, partners)
    first, beside = lax.optimization_barrier((first, beside))
    chips = [first, second, diagonal]
    return [spectrum, sibling] + chips + [exchange(chip, axis, 1) for chip in chips], beside


def per_device(records, travel_p, travel_s):
    groups, sensors, nodes = travel_p.shape
    count = 2 * groups * sensors
    parts = lax.axis_size("sens")
    width = nodes // parts
    limit = pltpu.CompilerParams(vmem_limit_bytes=24 << 20)
    table = pl.pallas_call(
        table_kernel,
        out_shape=jax.ShapeDtypeStruct((2, 3, HALF, 2 * BAND), jnp.bfloat16),
        compiler_params=limit,
        cost_estimate=pl.CostEstimate(flops=16 * HALF * 4 * BAND, bytes_accessed=0, transcendentals=0),
    )()
    spectrum = pl.pallas_call(
        forward_kernel,
        out_shape=jax.ShapeDtypeStruct((sensors, 4 * BAND), jnp.float32),
        compiler_params=limit,
    )(records[0], table)
    shifts = pl.pallas_call(
        functools.partial(shift_kernel, "grid", "sens"),
        out_shape=jax.ShapeDtypeStruct((parts, count, nodes), jnp.bfloat16),
        scratch_shapes=[pltpu.VMEM((parts, count, nodes), jnp.float32)],
        compiler_params=limit,
        cost_estimate=pl.CostEstimate(
            flops=parts * parts * count * nodes, bytes_accessed=4 * count * nodes, transcendentals=0
        ),
    )(travel_p, travel_s)
    spectra, shifts = gather_spectra(spectrum, "grid", shifts)
    functions = pl.pallas_call(
        function_kernel,
        out_shape=jax.ShapeDtypeStruct((SPAN, count), jnp.bfloat16),
        scratch_shapes=[pltpu.VMEM((SPAN, count), jnp.float32)],
        compiler_params=pltpu.CompilerParams(vmem_limit_bytes=28 << 20),
    )(*spectra, jnp.asarray(inverse_table()))

    def stack(offset, code, *extra):
        plain = jax.ShapeDtypeStruct((width, ANCHORS), jnp.float32)
        coded = jax.ShapeDtypeStruct((width, ANCHORS + 128), jnp.int16)
        return pl.pallas_call(
            functools.partial(stack_kernel, offset),
            out_shape=coded if code else plain,
            scratch_shapes=[
                pltpu.VMEM((COARSE * count, FINE // parts * nodes), jnp.bfloat16),
                pltpu.VMEM((ROWS, FINE // parts * nodes), jnp.float32),
                pltpu.VMEM((ANCHORS + 8, nodes), jnp.float32),
            ],
            compiler_params=pltpu.CompilerParams(vmem_limit_bytes=28 << 20),
            cost_estimate=pl.CostEstimate(flops=1024, bytes_accessed=1024, transcendentals=0),
        )(functions, shifts, *extra)

    if parts == 4:
        far = stack(3, True)
        passing = exchange(far, "sens", 1)
        functions, far = lax.optimization_barrier((functions, far))
        near = stack(1, True)
        nearby = exchange(near, "sens", 1)
        functions, near = lax.optimization_barrier((functions, near))
        crossing = exchange(stack(2, True, passing), "sens", 2)
        total = stack(0, False, nearby) + decode(crossing)
    else:
        arrived = [exchange(stack(offset, False), "sens", offset) for offset in range(1, parts)]
        total = stack(0, False)
        for part in arrived:
            total = total + part
    sensor_total = sensors * lax.axis_size("grid") * parts
    return total * (1.0 / math.sqrt(2.0 * sensor_total))


def solution(mesh):
    return jax.shard_map(
        per_device,
        mesh=mesh,
        in_specs=(P("grid", "sens", None), P(None, "sens", "grid"), P(None, "sens", "grid")),
        out_specs=P(("grid", "sens"), None),
        check_vma=False,
    )
```

```python
import functools
import math

import jax
import jax.numpy as jnp
import ml_dtypes
import numpy as np
from jax import lax
from jax.experimental import pallas as pl
from jax.experimental.pallas import tpu as pltpu
from jax.sharding import PartitionSpec as P

NT = 2048
HALF = NT // 2
BAND = 128
P_LOW = 160
S_LOW = 48
LAGS = 64
ANCHORS = 1024
SPAN = 1088
FINE = 16
COARSE = LAGS // FINE
ROWS = ANCHORS + FINE
STEP = 32
LEVELS = 32000.0
CHUNKS = 4
CHUNK = SPAN // CHUNKS


def split_bf16(table, count):
    pieces = []
    rest = table.astype(np.float32)
    for _ in range(count):
        piece = rest.astype(ml_dtypes.bfloat16)
        pieces.append(piece)
        rest = rest - piece.astype(np.float32)
    return pieces


def inverse_table():
    times = np.arange(SPAN)
    columns = []
    for parity in (0, 1):
        bins = np.arange(parity, BAND, 2)
        angles = 2.0 * np.pi * ((times[:, None] * bins[None, :]) % NT) / NT
        columns += [np.cos(angles), np.sin(angles)]
    return np.concatenate(split_bf16(np.concatenate(columns, 1) * (2.0 / NT), 2), 1)


def split_value(value, count):
    pieces = []
    for _ in range(count):
        piece = value.astype(jnp.bfloat16)
        pieces.append(piece)
        value = value - piece.astype(jnp.float32)
    return pieces


def dot(a, b, contract=((1,), (0,))):
    return lax.dot_general(a, b, (contract, ((), ())), preferred_element_type=jnp.float32)


def group_order(size, here):
    if size != 8:
        return [here ^ offset for offset in range(size)]
    near = 2 + 2 * (here & 1)
    far = 6 - near
    mine = [here, here ^ 1, here ^ near, here ^ near ^ 1, here ^ 6]
    return mine + [here ^ 1 ^ far, here ^ far, here ^ 7]


def shift_kernel(axis, owner_axis, shift_p_ref, shift_s_ref, out_ref, turned_ref):
    groups, block, nodes = shift_p_ref.shape
    parts = out_ref.shape[0]
    width = nodes // parts
    order = group_order(groups, lax.axis_index(axis))
    rows = [ref[group] for ref in (shift_p_ref, shift_s_ref) for group in order]
    shifts = jnp.concatenate(rows, axis=0).astype(jnp.float32)
    lane = lax.broadcasted_iota(jnp.int32, shifts.shape, 1) // width
    for turn in range(parts):
        turned_ref[turn] = pltpu.roll(shifts, turn * width, 1) if turn else shifts
    owner = lax.axis_index(owner_axis)
    for offset in range(parts):
        target = owner ^ offset
        spread = turned_ref[(parts - target) & (parts - 1)]
        for place in range(1, parts):
            turned = turned_ref[(place - target) & (parts - 1)]
            spread = jnp.where(lane == place, turned, spread)
        out_ref[offset] = (spread - lane.astype(jnp.float32)).astype(jnp.bfloat16)


def table_kernel(table_ref):
    half = BAND // 2
    lane = lax.broadcasted_iota(jnp.int32, (STEP, BAND), 1)
    row = lax.broadcasted_iota(jnp.int32, (STEP, BAND), 0)
    bins = jnp.where(lane < half, P_LOW + 2 * lane, S_LOW + 2 * (lane - half))
    for parity in (0, 1):
        fine = ((row * (bins + parity)) & (NT - 1)).astype(jnp.float32) * (2.0 * math.pi / NT)
        base = ((row * STEP * (bins + parity)) & (NT - 1)).astype(jnp.float32) * (2.0 * math.pi / NT)
        fine_cos, fine_sin = jnp.cos(fine), jnp.sin(fine)
        base_cos, base_sin = jnp.cos(base), jnp.sin(base)
        for step in range(HALF // STEP):
            step_cos, step_sin = base_cos[step : step + 1], base_sin[step : step + 1]
            rows = slice(step * STEP, (step + 1) * STEP)
            for column, value in (
                (0, step_cos * fine_cos - step_sin * fine_sin),
                (BAND, step_sin * fine_cos + step_cos * fine_sin),
            ):
                for index, piece in enumerate(split_value(value, 3)):
                    table_ref[parity, index, rows, column : column + BAND] = piece


def forward_kernel(*refs):
    blocks = len(refs) // 2
    record_refs, table_ref, out_refs = refs[:blocks], refs[blocks], refs[blocks + 1 :]
    records = jnp.concatenate([ref[...] for ref in record_refs], axis=0)
    sensors = records.shape[0]
    half = BAND // 2
    early, late = records[:, :HALF], records[:, HALF:]
    for parity, folded in ((0, early + late), (1, early - late)):
        pieces = split_value(folded, 3)
        total = None
        for index in (2, 1, 0):
            stacked = jnp.concatenate(pieces[: 3 - index], axis=0)
            product = dot(stacked, table_ref[parity, index])
            for part in reversed(range(3 - index)):
                term = product[part * sensors : (part + 1) * sensors]
                total = term if total is None else total + term
        for band in range(2):
            column = (2 * band + parity) * BAND
            for side in range(2):
                first = side * BAND + band * half
                for ref in out_refs:
                    rows = ref.shape[0]
                    columns = slice(column + side * half, column + (side + 1) * half)
                    ref[:, columns] = total[:rows, first : first + half]


def function_kernel(*refs):
    spectrum_refs, (table_ref, out_ref, envelope_ref) = refs[:-3], refs[-3:]
    count = out_ref.shape[1]
    spectrum = jnp.concatenate([ref[...] for ref in spectrum_refs], axis=0)
    spectrum = jnp.concatenate([spectrum[:, : 2 * BAND], spectrum[:, 2 * BAND :]], axis=0)
    half = BAND // 2
    blocks = []
    for first in (0, BAND):
        block = pltpu.roll(spectrum[:, first : first + BAND], half, 1)
        lane = lax.broadcasted_iota(jnp.int32, block.shape, 1)
        blocks.append(jnp.where(lane < half, -block, block))
    spectrum = jnp.concatenate([spectrum, jnp.concatenate(blocks, axis=1)], axis=0)
    high, low = split_value(spectrum, 2)
    weights = jnp.concatenate([high, low, high], axis=1)
    total = jnp.zeros((1, count), jnp.float32)
    for chunk in range(CHUNKS):
        table = table_ref[chunk * CHUNK : (chunk + 1) * CHUNK, :]
        left = jnp.concatenate([table[:, : 2 * BAND], table], axis=1)
        analytic = dot(left, weights, ((1,), (1,)))
        real, imag = analytic[:, :count], analytic[:, count:]
        power = real * real + imag * imag + 1e-06
        envelope = power * lax.rsqrt(power)
        envelope_ref[chunk * CHUNK : (chunk + 1) * CHUNK, :] = envelope
        total = total + jnp.sum(envelope, axis=0, keepdims=True)
    scale = 1.0 / (total * (1.0 / SPAN))
    out_ref[...] = (envelope_ref[...] * scale - 1.0).astype(jnp.bfloat16)


def step_size(code):
    return jnp.exp2(code * 0.125) * (1.0 / LEVELS)


def encode(value):
    largest = jnp.max(jnp.abs(value), axis=1, keepdims=True)
    code = jnp.floor(8.0 * jnp.log2(jnp.maximum(largest, 1e-30))) + 1.0
    levels = jnp.round(value * (1.0 / step_size(code))).astype(jnp.int32)
    codes = jnp.broadcast_to(code, (value.shape[0], 128)).astype(jnp.int32)
    return jnp.concatenate([levels, codes], axis=1).astype(jnp.int16)


def decode(coded):
    columns = coded.shape[1] - 128
    code = coded[:, columns : columns + 1].astype(jnp.float32)
    return coded[:, :columns].astype(jnp.float32) * step_size(code)


def stack_kernel(offset, functions_ref, shifts_ref, *refs):
    extra_refs, (out_ref, sums_ref, near_ref) = refs[:-3], refs[-3:]
    parts, count, nodes = shifts_ref.shape
    blocks = FINE // parts
    width = nodes // parts
    shifts = shifts_ref[offset]
    one = jnp.ones((), jnp.bfloat16)
    zero = jnp.zeros((), jnp.bfloat16)
    lagged = [functions_ref[c * FINE : c * FINE + ROWS, :] for c in range(COARSE)]
    lagged = jnp.concatenate(lagged, axis=1)

    def hot(coarse, block):
        lag = jnp.bfloat16(coarse * FINE + block * parts)
        return jnp.where(shifts == lag, one, zero)

    step = min(2, blocks)
    for first in range(0, blocks, step):
        rows = []
        for coarse in range(COARSE):
            rows.append(jnp.concatenate([hot(coarse, first + k) for k in range(step)], axis=1))
        columns = slice(first * nodes, (first + step) * nodes)
        sums_ref[:, columns] = dot(lagged, jnp.concatenate(rows, axis=0))
    for first, rows in ((0, ANCHORS), (ANCHORS, parts)):
        near = None
        for block in range(blocks):
            row = first + block * parts
            term = sums_ref[row : row + rows, block * nodes : (block + 1) * nodes]
            near = term if near is None else near + term
        near_ref[first : first + rows, :] = near
    lane = lax.broadcasted_iota(jnp.int32, (ANCHORS, nodes), 1) // width
    total = near_ref[:ANCHORS, :]
    for place in range(1, parts):
        total = jnp.where(lane == place, near_ref[place : place + ANCHORS, :], total)
    turned = total.T
    result = turned[:width]
    for place in range(1, parts):
        result = result + turned[place * width : (place + 1) * width]
    for ref in extra_refs:
        result = result + decode(ref[...])
    out_ref[...] = encode(result) if out_ref.dtype == jnp.int16 else result


def exchange(value, axis, offset):
    size = lax.axis_size(axis)
    return lax.ppermute(value, axis, [(i, i ^ offset) for i in range(size)])


def gather_spectra(forward, records, axis, beside):
    size = lax.axis_size(axis)
    if size != 8:
        (spectrum,) = forward(records)
        return [spectrum] + [exchange(spectrum, axis, offset) for offset in range(1, size)], beside
    chip, own = forward(records, exchange(records, axis, 1))
    diagonal = exchange(own, axis, 6)
    near = lax.ppermute(chip, axis, [(i, i ^ (2 + 2 * (i & 1))) for i in range(size)])
    near, beside = lax.optimization_barrier((near, beside))
    return [chip, near, diagonal, exchange(near, axis, 1), exchange(diagonal, axis, 1)], beside


def per_device(records, travel_p, travel_s):
    groups, sensors, nodes = travel_p.shape
    count = 2 * groups * sensors
    parts = lax.axis_size("sens")
    width = nodes // parts
    limit = pltpu.CompilerParams(vmem_limit_bytes=24 << 20)
    table = pl.pallas_call(
        table_kernel,
        out_shape=jax.ShapeDtypeStruct((2, 3, HALF, 2 * BAND), jnp.bfloat16),
        compiler_params=limit,
        cost_estimate=pl.CostEstimate(flops=16 * HALF * 4 * BAND, bytes_accessed=0, transcendentals=0),
    )()

    def forward(*blocks):
        sizes = [len(blocks) * sensors, sensors][: len(blocks)]
        return pl.pallas_call(
            forward_kernel,
            out_shape=[jax.ShapeDtypeStruct((size, 4 * BAND), jnp.float32) for size in sizes],
            compiler_params=limit,
        )(*blocks, table)

    shifts = pl.pallas_call(
        functools.partial(shift_kernel, "grid", "sens"),
        out_shape=jax.ShapeDtypeStruct((parts, count, nodes), jnp.bfloat16),
        scratch_shapes=[pltpu.VMEM((parts, count, nodes), jnp.float32)],
        compiler_params=limit,
        cost_estimate=pl.CostEstimate(
            flops=parts * parts * count * nodes, bytes_accessed=4 * count * nodes, transcendentals=0
        ),
    )(travel_p, travel_s)
    spectra, shifts = gather_spectra(forward, records[0], "grid", shifts)
    functions = pl.pallas_call(
        function_kernel,
        out_shape=jax.ShapeDtypeStruct((SPAN, count), jnp.bfloat16),
        scratch_shapes=[pltpu.VMEM((SPAN, count), jnp.float32)],
        compiler_params=pltpu.CompilerParams(vmem_limit_bytes=28 << 20),
    )(*spectra, jnp.asarray(inverse_table()))

    def stack(offset, code, *extra):
        plain = jax.ShapeDtypeStruct((width, ANCHORS), jnp.float32)
        coded = jax.ShapeDtypeStruct((width, ANCHORS + 128), jnp.int16)
        return pl.pallas_call(
            functools.partial(stack_kernel, offset),
            out_shape=coded if code else plain,
            scratch_shapes=[
                pltpu.VMEM((ROWS, FINE // parts * nodes), jnp.float32),
                pltpu.VMEM((ANCHORS + 8, nodes), jnp.float32),
            ],
            compiler_params=pltpu.CompilerParams(vmem_limit_bytes=28 << 20),
            cost_estimate=pl.CostEstimate(flops=1024, bytes_accessed=1024, transcendentals=0),
        )(functions, shifts, *extra)

    if parts == 4:
        far = stack(3, True)
        passing = exchange(far, "sens", 1)
        functions, far = lax.optimization_barrier((functions, far))
        near = stack(1, True)
        nearby = exchange(near, "sens", 1)
        functions, near = lax.optimization_barrier((functions, near))
        crossing = exchange(stack(2, True, passing), "sens", 2)
        total = stack(0, False, nearby) + decode(crossing)
    else:
        arrived = [exchange(stack(offset, False), "sens", offset) for offset in range(1, parts)]
        total = stack(0, False)
        for part in arrived:
            total = total + part
    sensor_total = sensors * lax.axis_size("grid") * parts
    return total * (1.0 / math.sqrt(2.0 * sensor_total))


def solution(mesh):
    return jax.shard_map(
        per_device,
        mesh=mesh,
        in_specs=(P("grid", "sens", None), P(None, "sens", "grid"), P(None, "sens", "grid")),
        out_specs=P(("grid", "sens"), None),
        check_vma=False,
    )
```

```python
import functools
import math

import jax
import jax.numpy as jnp
import ml_dtypes
import numpy as np
from jax import lax
from jax.experimental import pallas as pl
from jax.experimental.pallas import tpu as pltpu
from jax.sharding import PartitionSpec as P

NT = 2048
HALF = NT // 2
BAND = 128
P_LOW = 160
S_LOW = 48
LAGS = 64
ANCHORS = 1024
SPAN = 1088
FINE = 16
COARSE = LAGS // FINE
ROWS = ANCHORS + FINE
STEP = 32
LEVELS = 32000.0
CHUNKS = 4
CHUNK = SPAN // CHUNKS


def split_bf16(table, count):
    pieces = []
    rest = table.astype(np.float32)
    for _ in range(count):
        piece = rest.astype(ml_dtypes.bfloat16)
        pieces.append(piece)
        rest = rest - piece.astype(np.float32)
    return pieces


def inverse_table():
    times = np.arange(SPAN)
    columns = []
    for parity in (0, 1):
        bins = np.arange(parity, BAND, 2)
        angles = 2.0 * np.pi * ((times[:, None] * bins[None, :]) % NT) / NT
        columns += [np.cos(angles), np.sin(angles)]
    return np.concatenate(split_bf16(np.concatenate(columns, 1) * (2.0 / NT), 2), 1)


def split_value(value, count):
    pieces = []
    for _ in range(count):
        piece = value.astype(jnp.bfloat16)
        pieces.append(piece)
        value = value - piece.astype(jnp.float32)
    return pieces


def dot(a, b, contract=((1,), (0,))):
    return lax.dot_general(a, b, (contract, ((), ())), preferred_element_type=jnp.float32)


def group_order(size, here):
    if size != 8:
        return [here ^ offset for offset in range(size)]
    near = 2 + 2 * (here & 1)
    far = 6 - near
    mine = [here, here ^ 1, here ^ near, here ^ near ^ 1, here ^ 6]
    return mine + [here ^ 1 ^ far, here ^ far, here ^ 7]


def shift_kernel(axis, owner_axis, shift_p_ref, shift_s_ref, out_ref, turned_ref):
    groups, block, nodes = shift_p_ref.shape
    parts = out_ref.shape[0]
    width = nodes // parts
    order = group_order(groups, lax.axis_index(axis))
    halves = [order[:4], order[4:]] if groups == 8 else [order]
    refs = (shift_p_ref, shift_s_ref)
    rows = [ref[group] for half in halves for ref in refs for group in half]
    shifts = jnp.concatenate(rows, axis=0).astype(jnp.float32)
    lane = lax.broadcasted_iota(jnp.int32, shifts.shape, 1) // width
    for turn in range(parts):
        turned_ref[turn] = pltpu.roll(shifts, turn * width, 1) if turn else shifts
    owner = lax.axis_index(owner_axis)
    for offset in range(parts):
        target = owner ^ offset
        spread = turned_ref[(parts - target) & (parts - 1)]
        for place in range(1, parts):
            turned = turned_ref[(place - target) & (parts - 1)]
            spread = jnp.where(lane == place, turned, spread)
        out_ref[offset] = (spread - lane.astype(jnp.float32)).astype(jnp.bfloat16)


def table_kernel(table_ref):
    half = BAND // 2
    lane = lax.broadcasted_iota(jnp.int32, (STEP, BAND), 1)
    row = lax.broadcasted_iota(jnp.int32, (STEP, BAND), 0)
    bins = jnp.where(lane < half, P_LOW + 2 * lane, S_LOW + 2 * (lane - half))
    for parity in (0, 1):
        fine = ((row * (bins + parity)) & (NT - 1)).astype(jnp.float32) * (2.0 * math.pi / NT)
        base = ((row * STEP * (bins + parity)) & (NT - 1)).astype(jnp.float32) * (2.0 * math.pi / NT)
        fine_cos, fine_sin = jnp.cos(fine), jnp.sin(fine)
        base_cos, base_sin = jnp.cos(base), jnp.sin(base)
        for step in range(HALF // STEP):
            step_cos, step_sin = base_cos[step : step + 1], base_sin[step : step + 1]
            rows = slice(step * STEP, (step + 1) * STEP)
            for column, value in (
                (0, step_cos * fine_cos - step_sin * fine_sin),
                (BAND, step_sin * fine_cos + step_cos * fine_sin),
            ):
                for index, piece in enumerate(split_value(value, 3)):
                    table_ref[parity, index, rows, column : column + BAND] = piece


def forward_kernel(*refs):
    blocks = len(refs) // 2
    record_refs, table_ref, out_refs = refs[:blocks], refs[blocks], refs[blocks + 1 :]
    records = jnp.concatenate([ref[...] for ref in record_refs], axis=0)
    sensors = records.shape[0]
    half = BAND // 2
    early, late = records[:, :HALF], records[:, HALF:]
    for parity, folded in ((0, early + late), (1, early - late)):
        pieces = split_value(folded, 3)
        total = None
        for index in (2, 1, 0):
            stacked = jnp.concatenate(pieces[: 3 - index], axis=0)
            product = dot(stacked, table_ref[parity, index])
            for part in reversed(range(3 - index)):
                term = product[part * sensors : (part + 1) * sensors]
                total = term if total is None else total + term
        for band in range(2):
            column = (2 * band + parity) * BAND
            for side in range(2):
                first = side * BAND + band * half
                for ref in out_refs:
                    rows = ref.shape[0]
                    columns = slice(column + side * half, column + (side + 1) * half)
                    ref[:, columns] = total[:rows, first : first + half]


def function_kernel(*refs):
    spectrum_refs, (table_ref, out_ref, envelope_ref) = refs[:-3], refs[-3:]
    count = out_ref.shape[1]
    spectrum = jnp.concatenate([ref[...] for ref in spectrum_refs], axis=0)
    spectrum = jnp.concatenate([spectrum[:, : 2 * BAND], spectrum[:, 2 * BAND :]], axis=0)
    half = BAND // 2
    blocks = []
    for first in (0, BAND):
        block = pltpu.roll(spectrum[:, first : first + BAND], half, 1)
        lane = lax.broadcasted_iota(jnp.int32, block.shape, 1)
        blocks.append(jnp.where(lane < half, -block, block))
    spectrum = jnp.concatenate([spectrum, jnp.concatenate(blocks, axis=1)], axis=0)
    high, low = split_value(spectrum, 2)
    weights = jnp.concatenate([high, low, high], axis=1)
    total = jnp.zeros((1, count), jnp.float32)
    for chunk in range(CHUNKS):
        table = table_ref[chunk * CHUNK : (chunk + 1) * CHUNK, :]
        left = jnp.concatenate([table[:, : 2 * BAND], table], axis=1)
        analytic = dot(left, weights, ((1,), (1,)))
        real, imag = analytic[:, :count], analytic[:, count:]
        power = real * real + imag * imag + 1e-06
        envelope = power * lax.rsqrt(power)
        envelope_ref[chunk * CHUNK : (chunk + 1) * CHUNK, :] = envelope
        total = total + jnp.sum(envelope, axis=0, keepdims=True)
    scale = 1.0 / (total * (1.0 / SPAN))
    out_ref[...] = (envelope_ref[...] * scale - 1.0).astype(jnp.bfloat16)


def step_size(code):
    return jnp.exp2(code * 0.125) * (1.0 / LEVELS)


def encode(value):
    largest = jnp.max(jnp.abs(value), axis=1, keepdims=True)
    code = jnp.floor(8.0 * jnp.log2(jnp.maximum(largest, 1e-30))) + 1.0
    levels = jnp.round(value * (1.0 / step_size(code))).astype(jnp.int32)
    codes = jnp.broadcast_to(code, (value.shape[0], 128)).astype(jnp.int32)
    return jnp.concatenate([levels, codes], axis=1).astype(jnp.int16)


def decode(coded):
    columns = coded.shape[1] - 128
    code = coded[:, columns : columns + 1].astype(jnp.float32)
    return coded[:, :columns].astype(jnp.float32) * step_size(code)


def stack_kernel(offset, pieces, shifts_ref, *refs):
    functions_refs, extra_refs, (out_ref, sums_ref, near_ref) = refs[:pieces], refs[pieces:-3], refs[-3:]
    parts, count, nodes = shifts_ref.shape
    blocks = FINE // parts
    width = nodes // parts
    shifts = shifts_ref[offset]
    one = jnp.ones((), jnp.bfloat16)
    zero = jnp.zeros((), jnp.bfloat16)
    lagged = [ref[c * FINE : c * FINE + ROWS, :] for c in range(COARSE) for ref in functions_refs]
    lagged = jnp.concatenate(lagged, axis=1)

    def hot(coarse, block):
        lag = jnp.bfloat16(coarse * FINE + block * parts)
        return jnp.where(shifts == lag, one, zero)

    step = min(2, blocks)
    for first in range(0, blocks, step):
        rows = []
        for coarse in range(COARSE):
            rows.append(jnp.concatenate([hot(coarse, first + k) for k in range(step)], axis=1))
        columns = slice(first * nodes, (first + step) * nodes)
        sums_ref[:, columns] = dot(lagged, jnp.concatenate(rows, axis=0))
    for first, rows in ((0, ANCHORS), (ANCHORS, parts)):
        near = None
        for block in range(blocks):
            row = first + block * parts
            term = sums_ref[row : row + rows, block * nodes : (block + 1) * nodes]
            near = term if near is None else near + term
        near_ref[first : first + rows, :] = near
    lane = lax.broadcasted_iota(jnp.int32, (ANCHORS, nodes), 1) // width
    total = near_ref[:ANCHORS, :]
    for place in range(1, parts):
        total = jnp.where(lane == place, near_ref[place : place + ANCHORS, :], total)
    turned = total.T
    result = turned[:width]
    for place in range(1, parts):
        result = result + turned[place * width : (place + 1) * width]
    for ref in extra_refs:
        result = result + decode(ref[...])
    out_ref[...] = encode(result) if out_ref.dtype == jnp.int16 else result


def exchange(value, axis, offset):
    size = lax.axis_size(axis)
    return lax.ppermute(value, axis, [(i, i ^ offset) for i in range(size)])


def gather_spectra(forward, records, axis, beside):
    size = lax.axis_size(axis)
    if size != 8:
        (spectrum,) = forward(records)
        return [[spectrum] + [exchange(spectrum, axis, offset) for offset in range(1, size)]], beside
    chip, own = forward(records, exchange(records, axis, 1))
    diagonal = exchange(own, axis, 6)
    near = lax.ppermute(chip, axis, [(i, i ^ (2 + 2 * (i & 1))) for i in range(size)])
    near, beside = lax.optimization_barrier((near, beside))
    return [[chip, near], [diagonal, exchange(near, axis, 1), exchange(diagonal, axis, 1)]], beside


def per_device(records, travel_p, travel_s):
    groups, sensors, nodes = travel_p.shape
    count = 2 * groups * sensors
    parts = lax.axis_size("sens")
    width = nodes // parts
    limit = pltpu.CompilerParams(vmem_limit_bytes=24 << 20)
    table = pl.pallas_call(
        table_kernel,
        out_shape=jax.ShapeDtypeStruct((2, 3, HALF, 2 * BAND), jnp.bfloat16),
        compiler_params=limit,
        cost_estimate=pl.CostEstimate(flops=16 * HALF * 4 * BAND, bytes_accessed=0, transcendentals=0),
    )()

    def forward(*blocks):
        sizes = [len(blocks) * sensors, sensors][: len(blocks)]
        return pl.pallas_call(
            forward_kernel,
            out_shape=[jax.ShapeDtypeStruct((size, 4 * BAND), jnp.float32) for size in sizes],
            compiler_params=limit,
        )(*blocks, table)

    shifts = pl.pallas_call(
        functools.partial(shift_kernel, "grid", "sens"),
        out_shape=jax.ShapeDtypeStruct((parts, count, nodes), jnp.bfloat16),
        scratch_shapes=[pltpu.VMEM((parts, count, nodes), jnp.float32)],
        compiler_params=limit,
        cost_estimate=pl.CostEstimate(
            flops=parts * parts * count * nodes, bytes_accessed=4 * count * nodes, transcendentals=0
        ),
    )(travel_p, travel_s)
    spectra, shifts = gather_spectra(forward, records[0], "grid", shifts)
    inverse = jnp.asarray(inverse_table())

    def rebuild(blocks):
        columns = 2 * sum(block.shape[0] for block in blocks)
        return pl.pallas_call(
            function_kernel,
            out_shape=jax.ShapeDtypeStruct((SPAN, columns), jnp.bfloat16),
            scratch_shapes=[pltpu.VMEM((SPAN, columns), jnp.float32)],
            compiler_params=pltpu.CompilerParams(vmem_limit_bytes=28 << 20),
            cost_estimate=pl.CostEstimate(
                flops=12 * SPAN * 2 * BAND * columns,
                bytes_accessed=2 * SPAN * columns,
                transcendentals=SPAN * columns,
            ),
        )(*blocks, inverse)

    functions = tuple(rebuild(blocks) for blocks in spectra)

    def stack(offset, code, *extra):
        plain = jax.ShapeDtypeStruct((width, ANCHORS), jnp.float32)
        coded = jax.ShapeDtypeStruct((width, ANCHORS + 128), jnp.int16)
        return pl.pallas_call(
            functools.partial(stack_kernel, offset, len(functions)),
            out_shape=coded if code else plain,
            scratch_shapes=[
                pltpu.VMEM((ROWS, FINE // parts * nodes), jnp.float32),
                pltpu.VMEM((ANCHORS + 8, nodes), jnp.float32),
            ],
            compiler_params=pltpu.CompilerParams(vmem_limit_bytes=28 << 20),
            cost_estimate=pl.CostEstimate(flops=1024, bytes_accessed=1024, transcendentals=0),
        )(shifts, *functions, *extra)

    if parts == 4:
        far = stack(3, True)
        passing = exchange(far, "sens", 1)
        functions, far = lax.optimization_barrier((functions, far))
        near = stack(1, True)
        nearby = exchange(near, "sens", 1)
        functions, near = lax.optimization_barrier((functions, near))
        crossing = exchange(stack(2, True, passing), "sens", 2)
        total = stack(0, False, nearby) + decode(crossing)
    else:
        arrived = [exchange(stack(offset, False), "sens", offset) for offset in range(1, parts)]
        total = stack(0, False)
        for part in arrived:
            total = total + part
    sensor_total = sensors * lax.axis_size("grid") * parts
    return total * (1.0 / math.sqrt(2.0 * sensor_total))


def solution(mesh):
    return jax.shard_map(
        per_device,
        mesh=mesh,
        in_specs=(P("grid", "sens", None), P(None, "sens", "grid"), P(None, "sens", "grid")),
        out_specs=P(("grid", "sens"), None),
        check_vma=False,
    )
```

```python
import functools
import math

import jax
import jax.numpy as jnp
import ml_dtypes
import numpy as np
from jax import lax
from jax.experimental import pallas as pl
from jax.experimental.pallas import tpu as pltpu
from jax.sharding import PartitionSpec as P

NT = 2048
HALF = NT // 2
BAND = 128
P_LOW = 160
S_LOW = 48
LAGS = 64
ANCHORS = 1024
SPAN = 1088
FINE = 16
COARSE = LAGS // FINE
ROWS = ANCHORS + FINE
STEP = 32
LEVELS = 32000.0
CHUNKS = 4
CHUNK = SPAN // CHUNKS


def split_bf16(table, count):
    pieces = []
    rest = table.astype(np.float32)
    for _ in range(count):
        piece = rest.astype(ml_dtypes.bfloat16)
        pieces.append(piece)
        rest = rest - piece.astype(np.float32)
    return pieces


def inverse_table():
    times = np.arange(SPAN)
    columns = []
    for parity in (0, 1):
        bins = np.arange(parity, BAND, 2)
        angles = 2.0 * np.pi * ((times[:, None] * bins[None, :]) % NT) / NT
        columns += [np.cos(angles), np.sin(angles)]
    return np.concatenate(split_bf16(np.concatenate(columns, 1) * (2.0 / NT), 2), 1)


def split_value(value, count):
    pieces = []
    for _ in range(count):
        piece = value.astype(jnp.bfloat16)
        pieces.append(piece)
        value = value - piece.astype(jnp.float32)
    return pieces


def dot(a, b, contract=((1,), (0,))):
    return lax.dot_general(a, b, (contract, ((), ())), preferred_element_type=jnp.float32)


def group_order(size, here):
    if size != 8:
        return [here ^ offset for offset in range(size)]
    near = 2 + 2 * (here & 1)
    far = 6 - near
    mine = [here, here ^ 1, here ^ near, here ^ near ^ 1, here ^ 6]
    return mine + [here ^ 1 ^ far, here ^ far, here ^ 7]


def shift_kernel(axis, owner_axis, shift_p_ref, shift_s_ref, out_ref, turned_ref):
    groups, block, nodes = shift_p_ref.shape
    parts = out_ref.shape[0]
    width = nodes // parts
    order = group_order(groups, lax.axis_index(axis))
    halves = [order[:4], order[4:]] if groups == 8 else [order]
    refs = (shift_p_ref, shift_s_ref)
    rows = [ref[group] for half in halves for ref in refs for group in half]
    shifts = jnp.concatenate(rows, axis=0).astype(jnp.float32)
    lane = lax.broadcasted_iota(jnp.int32, shifts.shape, 1) // width
    for turn in range(parts):
        turned_ref[turn] = pltpu.roll(shifts, turn * width, 1) if turn else shifts
    owner = lax.axis_index(owner_axis)
    for offset in range(parts):
        target = owner ^ offset
        spread = turned_ref[(parts - target) & (parts - 1)]
        for place in range(1, parts):
            turned = turned_ref[(place - target) & (parts - 1)]
            spread = jnp.where(lane == place, turned, spread)
        out_ref[offset] = (spread - lane.astype(jnp.float32)).astype(jnp.bfloat16)


def table_kernel(table_ref):
    half = BAND // 2
    lane = lax.broadcasted_iota(jnp.int32, (STEP, BAND), 1)
    row = lax.broadcasted_iota(jnp.int32, (STEP, BAND), 0)
    bins = jnp.where(lane < half, P_LOW + 2 * lane, S_LOW + 2 * (lane - half))
    for parity in (0, 1):
        fine = ((row * (bins + parity)) & (NT - 1)).astype(jnp.float32) * (2.0 * math.pi / NT)
        base = ((row * STEP * (bins + parity)) & (NT - 1)).astype(jnp.float32) * (2.0 * math.pi / NT)
        fine_cos, fine_sin = jnp.cos(fine), jnp.sin(fine)
        base_cos, base_sin = jnp.cos(base), jnp.sin(base)
        for step in range(HALF // STEP):
            step_cos, step_sin = base_cos[step : step + 1], base_sin[step : step + 1]
            rows = slice(step * STEP, (step + 1) * STEP)
            for column, value in (
                (0, step_cos * fine_cos - step_sin * fine_sin),
                (BAND, step_sin * fine_cos + step_cos * fine_sin),
            ):
                for index, piece in enumerate(split_value(value, 3)):
                    table_ref[parity, index, rows, column : column + BAND] = piece


def forward_kernel(*refs):
    blocks = len(refs) // 2
    record_refs, table_ref, out_refs = refs[:blocks], refs[blocks], refs[blocks + 1 :]
    records = jnp.concatenate([ref[...] for ref in record_refs], axis=0)
    sensors = records.shape[0]
    half = BAND // 2
    early, late = records[:, :HALF], records[:, HALF:]
    for parity, folded in ((0, early + late), (1, early - late)):
        pieces = split_value(folded, 3)
        total = None
        for index in (2, 1, 0):
            stacked = jnp.concatenate(pieces[: 3 - index], axis=0)
            product = dot(stacked, table_ref[parity, index])
            for part in reversed(range(3 - index)):
                term = product[part * sensors : (part + 1) * sensors]
                total = term if total is None else total + term
        for band in range(2):
            column = (2 * band + parity) * BAND
            for side in range(2):
                first = side * BAND + band * half
                for ref in out_refs:
                    rows = ref.shape[0]
                    columns = slice(column + side * half, column + (side + 1) * half)
                    ref[:, columns] = total[:rows, first : first + half]


def function_kernel(*refs):
    spectrum_refs, (table_ref, out_ref, envelope_ref) = refs[:-3], refs[-3:]
    count = out_ref.shape[1]
    spectrum = jnp.concatenate([ref[...] for ref in spectrum_refs], axis=0)
    spectrum = jnp.concatenate([spectrum[:, : 2 * BAND], spectrum[:, 2 * BAND :]], axis=0)
    half = BAND // 2
    blocks = []
    for first in (0, BAND):
        block = pltpu.roll(spectrum[:, first : first + BAND], half, 1)
        lane = lax.broadcasted_iota(jnp.int32, block.shape, 1)
        blocks.append(jnp.where(lane < half, -block, block))
    spectrum = jnp.concatenate([spectrum, jnp.concatenate(blocks, axis=1)], axis=0)
    high, low = split_value(spectrum, 2)
    weights = jnp.concatenate([high, low, high], axis=1)
    total = jnp.zeros((1, count), jnp.float32)
    for chunk in range(CHUNKS):
        table = table_ref[chunk * CHUNK : (chunk + 1) * CHUNK, :]
        left = jnp.concatenate([table[:, : 2 * BAND], table], axis=1)
        analytic = dot(left, weights, ((1,), (1,)))
        real, imag = analytic[:, :count], analytic[:, count:]
        power = real * real + imag * imag + 1e-06
        envelope = power * lax.rsqrt(power)
        envelope_ref[chunk * CHUNK : (chunk + 1) * CHUNK, :] = envelope
        total = total + jnp.sum(envelope, axis=0, keepdims=True)
    scale = 1.0 / (total * (1.0 / SPAN))
    out_ref[...] = (envelope_ref[...] * scale - 1.0).astype(jnp.bfloat16)


def step_size(code):
    return jnp.exp2(code * 0.125) * (1.0 / LEVELS)


def encode(value):
    largest = jnp.max(jnp.abs(value), axis=1, keepdims=True)
    code = jnp.floor(8.0 * jnp.log2(jnp.maximum(largest, 1e-30))) + 1.0
    levels = jnp.round(value * (1.0 / step_size(code))).astype(jnp.int32)
    codes = jnp.broadcast_to(code, (value.shape[0], 128)).astype(jnp.int32)
    return jnp.concatenate([levels, codes], axis=1).astype(jnp.int16)


def decode(coded):
    columns = coded.shape[1] - 128
    code = coded[:, columns : columns + 1].astype(jnp.float32)
    return coded[:, :columns].astype(jnp.float32) * step_size(code)


def stack_kernel(offset, pieces, shifts_ref, *refs):
    functions_refs, extra_refs, (out_ref, sums_ref, near_ref) = refs[:pieces], refs[pieces:-3], refs[-3:]
    parts, count, nodes = shifts_ref.shape
    blocks = FINE // parts
    width = nodes // parts
    shifts = shifts_ref[offset]
    one = jnp.ones((), jnp.bfloat16)
    zero = jnp.zeros((), jnp.bfloat16)
    lagged = [ref[c * FINE : c * FINE + ROWS, :] for c in range(COARSE) for ref in functions_refs]
    lagged = jnp.concatenate(lagged, axis=1)

    def hot(coarse, block):
        lag = jnp.bfloat16(coarse * FINE + block * parts)
        return jnp.where(shifts == lag, one, zero)

    step = min(2, blocks)
    for first in range(0, blocks, step):
        rows = []
        for coarse in range(COARSE):
            rows.append(jnp.concatenate([hot(coarse, first + k) for k in range(step)], axis=1))
        columns = slice(first * nodes, (first + step) * nodes)
        sums_ref[:, columns] = dot(lagged, jnp.concatenate(rows, axis=0))
    for first, rows in ((0, ANCHORS), (ANCHORS, parts)):
        near = None
        for block in range(blocks):
            row = first + block * parts
            term = sums_ref[row : row + rows, block * nodes : (block + 1) * nodes]
            near = term if near is None else near + term
        near_ref[first : first + rows, :] = near
    lane = lax.broadcasted_iota(jnp.int32, (ANCHORS, nodes), 1) // width
    total = near_ref[:ANCHORS, :]
    for place in range(1, parts):
        total = jnp.where(lane == place, near_ref[place : place + ANCHORS, :], total)
    turned = total.T
    result = turned[:width]
    for place in range(1, parts):
        result = result + turned[place * width : (place + 1) * width]
    for ref in extra_refs:
        result = result + decode(ref[...])
    out_ref[...] = encode(result) if out_ref.dtype == jnp.int16 else result


def merge_kernel(sum_ref, arrived_ref, out_ref):
    out_ref[...] = encode(sum_ref[...] + decode(arrived_ref[...]))


def finish_kernel(scale, own_ref, first_ref, second_ref, out_ref):
    out_ref[...] = (own_ref[...] + decode(first_ref[...]) + decode(second_ref[...])) * scale


def exchange(value, axis, offset):
    size = lax.axis_size(axis)
    return lax.ppermute(value, axis, [(i, i ^ offset) for i in range(size)])


def gather_spectra(forward, records, axis, beside):
    size = lax.axis_size(axis)
    if size != 8:
        (spectrum,) = forward(records)
        return [[spectrum] + [exchange(spectrum, axis, offset) for offset in range(1, size)]], beside
    chip, own = forward(records, exchange(records, axis, 1))
    diagonal = exchange(own, axis, 6)
    near = lax.ppermute(chip, axis, [(i, i ^ (2 + 2 * (i & 1))) for i in range(size)])
    near, beside = lax.optimization_barrier((near, beside))
    return [[chip, near], [diagonal, exchange(near, axis, 1), exchange(diagonal, axis, 1)]], beside


def per_device(records, travel_p, travel_s):
    groups, sensors, nodes = travel_p.shape
    count = 2 * groups * sensors
    parts = lax.axis_size("sens")
    width = nodes // parts
    limit = pltpu.CompilerParams(vmem_limit_bytes=24 << 20)
    table = pl.pallas_call(
        table_kernel,
        out_shape=jax.ShapeDtypeStruct((2, 3, HALF, 2 * BAND), jnp.bfloat16),
        compiler_params=limit,
        cost_estimate=pl.CostEstimate(flops=16 * HALF * 4 * BAND, bytes_accessed=0, transcendentals=0),
    )()

    def forward(*blocks):
        sizes = [len(blocks) * sensors, sensors][: len(blocks)]
        return pl.pallas_call(
            forward_kernel,
            out_shape=[jax.ShapeDtypeStruct((size, 4 * BAND), jnp.float32) for size in sizes],
            compiler_params=limit,
        )(*blocks, table)

    shifts = pl.pallas_call(
        functools.partial(shift_kernel, "grid", "sens"),
        out_shape=jax.ShapeDtypeStruct((parts, count, nodes), jnp.bfloat16),
        scratch_shapes=[pltpu.VMEM((parts, count, nodes), jnp.float32)],
        compiler_params=limit,
        cost_estimate=pl.CostEstimate(
            flops=parts * parts * count * nodes, bytes_accessed=4 * count * nodes, transcendentals=0
        ),
    )(travel_p, travel_s)
    spectra, shifts = gather_spectra(forward, records[0], "grid", shifts)
    inverse = jnp.asarray(inverse_table())

    def rebuild(blocks):
        columns = 2 * sum(block.shape[0] for block in blocks)
        return pl.pallas_call(
            function_kernel,
            out_shape=jax.ShapeDtypeStruct((SPAN, columns), jnp.bfloat16),
            scratch_shapes=[pltpu.VMEM((SPAN, columns), jnp.float32)],
            compiler_params=pltpu.CompilerParams(vmem_limit_bytes=28 << 20),
            cost_estimate=pl.CostEstimate(
                flops=12 * SPAN * 2 * BAND * columns,
                bytes_accessed=2 * SPAN * columns,
                transcendentals=SPAN * columns,
            ),
        )(*blocks, inverse)

    functions = tuple(rebuild(blocks) for blocks in spectra)

    def stack(offset, code, *extra):
        plain = jax.ShapeDtypeStruct((width, ANCHORS), jnp.float32)
        coded = jax.ShapeDtypeStruct((width, ANCHORS + 128), jnp.int16)
        return pl.pallas_call(
            functools.partial(stack_kernel, offset, len(functions)),
            out_shape=coded if code else plain,
            scratch_shapes=[
                pltpu.VMEM((ROWS, FINE // parts * nodes), jnp.float32),
                pltpu.VMEM((ANCHORS + 8, nodes), jnp.float32),
            ],
            compiler_params=pltpu.CompilerParams(vmem_limit_bytes=28 << 20),
            cost_estimate=pl.CostEstimate(flops=1024, bytes_accessed=1024, transcendentals=0),
        )(shifts, *functions, *extra)

    sensor_total = sensors * lax.axis_size("grid") * parts
    scale = 1.0 / math.sqrt(2.0 * sensor_total)
    if parts == 4:
        far = stack(3, True)
        passing = exchange(far, "sens", 2)
        functions, far = lax.optimization_barrier((functions, far))
        across = stack(2, True)
        crossing = exchange(across, "sens", 2)
        functions, across = lax.optimization_barrier((functions, across))
        merged = pl.pallas_call(
            merge_kernel,
            out_shape=jax.ShapeDtypeStruct((width, ANCHORS + 128), jnp.int16),
            compiler_params=limit,
        )(stack(1, False), passing)
        nearby = exchange(merged, "sens", 1)
        functions, merged = lax.optimization_barrier((functions, merged))
        own = stack(0, False)
        return pl.pallas_call(
            functools.partial(finish_kernel, scale),
            out_shape=jax.ShapeDtypeStruct((width, ANCHORS), jnp.float32),
            compiler_params=limit,
        )(own, crossing, nearby)

    arrived = [exchange(stack(offset, False), "sens", offset) for offset in range(1, parts)]
    total = stack(0, False)
    for part in arrived:
        total = total + part
    return total * scale


def solution(mesh):
    return jax.shard_map(
        per_device,
        mesh=mesh,
        in_specs=(P("grid", "sens", None), P(None, "sens", "grid"), P(None, "sens", "grid")),
        out_specs=P(("grid", "sens"), None),
        check_vma=False,
    )
```

```python
import functools
import math

import jax
import jax.numpy as jnp
import ml_dtypes
import numpy as np
from jax import lax
from jax.experimental import pallas as pl
from jax.experimental.pallas import tpu as pltpu
from jax.sharding import PartitionSpec as P

NT = 2048
HALF = NT // 2
BAND = 128
P_LOW = 160
S_LOW = 48
LAGS = 64
ANCHORS = 1024
SPAN = 1088
FINE = 16
COARSE = LAGS // FINE
ROWS = ANCHORS + FINE
STEP = 32
LEVELS = 32000.0
CHUNKS = 2
CHUNK = SPAN // CHUNKS


def split_bf16(table, count):
    pieces = []
    rest = table.astype(np.float32)
    for _ in range(count):
        piece = rest.astype(ml_dtypes.bfloat16)
        pieces.append(piece)
        rest = rest - piece.astype(np.float32)
    return pieces


def inverse_table():
    times = np.arange(SPAN)
    columns = []
    for parity in (0, 1):
        bins = np.arange(parity, BAND, 2)
        angles = 2.0 * np.pi * ((times[:, None] * bins[None, :]) % NT) / NT
        columns += [np.cos(angles), np.sin(angles)]
    return np.concatenate(split_bf16(np.concatenate(columns, 1) * (2.0 / NT), 2), 1)


def split_value(value, count):
    pieces = []
    for _ in range(count):
        piece = value.astype(jnp.bfloat16)
        pieces.append(piece)
        value = value - piece.astype(jnp.float32)
    return pieces


def dot(a, b, contract=((1,), (0,))):
    return lax.dot_general(a, b, (contract, ((), ())), preferred_element_type=jnp.float32)


def group_order(size, here):
    if size != 8:
        return [here ^ offset for offset in range(size)]
    near = 2 + 2 * (here & 1)
    far = 6 - near
    mine = [here, here ^ 1, here ^ near, here ^ near ^ 1, here ^ 6]
    return mine + [here ^ 1 ^ far, here ^ far, here ^ 7]


def shift_kernel(axis, owner_axis, shift_p_ref, shift_s_ref, out_ref, turned_ref):
    groups, block, nodes = shift_p_ref.shape
    parts = out_ref.shape[0]
    width = nodes // parts
    order = group_order(groups, lax.axis_index(axis))
    halves = [order[:4], order[4:]] if groups == 8 else [order]
    refs = (shift_p_ref, shift_s_ref)
    rows = [ref[group] for half in halves for ref in refs for group in half]
    shifts = jnp.concatenate(rows, axis=0).astype(jnp.float32)
    lane = lax.broadcasted_iota(jnp.int32, shifts.shape, 1) // width
    for turn in range(parts):
        turned_ref[turn] = pltpu.roll(shifts, turn * width, 1) if turn else shifts
    owner = lax.axis_index(owner_axis)
    for offset in range(parts):
        target = owner ^ offset
        spread = turned_ref[(parts - target) & (parts - 1)]
        for place in range(1, parts):
            turned = turned_ref[(place - target) & (parts - 1)]
            spread = jnp.where(lane == place, turned, spread)
        out_ref[offset] = (spread - lane.astype(jnp.float32)).astype(jnp.bfloat16)


def table_kernel(table_ref):
    half = BAND // 2
    lane = lax.broadcasted_iota(jnp.int32, (STEP, BAND), 1)
    row = lax.broadcasted_iota(jnp.int32, (STEP, BAND), 0)
    bins = jnp.where(lane < half, P_LOW + 2 * lane, S_LOW + 2 * (lane - half))
    for parity in (0, 1):
        fine = ((row * (bins + parity)) & (NT - 1)).astype(jnp.float32) * (2.0 * math.pi / NT)
        base = ((row * STEP * (bins + parity)) & (NT - 1)).astype(jnp.float32) * (2.0 * math.pi / NT)
        fine_cos, fine_sin = jnp.cos(fine), jnp.sin(fine)
        base_cos, base_sin = jnp.cos(base), jnp.sin(base)
        for step in range(HALF // STEP):
            step_cos, step_sin = base_cos[step : step + 1], base_sin[step : step + 1]
            rows = slice(step * STEP, (step + 1) * STEP)
            for column, value in (
                (0, step_cos * fine_cos - step_sin * fine_sin),
                (BAND, step_sin * fine_cos + step_cos * fine_sin),
            ):
                for index, piece in enumerate(split_value(value, 3)):
                    table_ref[parity, index, rows, column : column + BAND] = piece


def forward_kernel(*refs):
    blocks = len(refs) // 2
    record_refs, table_ref, out_refs = refs[:blocks], refs[blocks], refs[blocks + 1 :]
    records = jnp.concatenate([ref[...] for ref in record_refs], axis=0)
    sensors = records.shape[0]
    half = BAND // 2
    early, late = records[:, :HALF], records[:, HALF:]
    for parity, folded in ((0, early + late), (1, early - late)):
        pieces = split_value(folded, 3)
        total = None
        for index in (2, 1, 0):
            stacked = jnp.concatenate(pieces[: 3 - index], axis=0)
            product = dot(stacked, table_ref[parity, index])
            for part in reversed(range(3 - index)):
                term = product[part * sensors : (part + 1) * sensors]
                total = term if total is None else total + term
        for band in range(2):
            column = (2 * band + parity) * BAND
            for side in range(2):
                first = side * BAND + band * half
                for ref in out_refs:
                    rows = ref.shape[0]
                    columns = slice(column + side * half, column + (side + 1) * half)
                    ref[:, columns] = total[:rows, first : first + half]


def function_kernel(*refs):
    spectrum_refs, (table_ref, out_ref, envelope_ref) = refs[:-3], refs[-3:]
    count = out_ref.shape[1]
    spectrum = jnp.concatenate([ref[...] for ref in spectrum_refs], axis=0)
    spectrum = jnp.concatenate([spectrum[:, : 2 * BAND], spectrum[:, 2 * BAND :]], axis=0)
    half = BAND // 2
    blocks = []
    for first in (0, BAND):
        block = pltpu.roll(spectrum[:, first : first + BAND], half, 1)
        lane = lax.broadcasted_iota(jnp.int32, block.shape, 1)
        blocks.append(jnp.where(lane < half, -block, block))
    spectrum = jnp.concatenate([spectrum, jnp.concatenate(blocks, axis=1)], axis=0)
    high, low = split_value(spectrum, 2)
    weights = jnp.concatenate([high, low, high], axis=1)
    total = jnp.zeros((1, count), jnp.float32)
    for chunk in range(CHUNKS):
        table = table_ref[chunk * CHUNK : (chunk + 1) * CHUNK, :]
        left = jnp.concatenate([table[:, : 2 * BAND], table], axis=1)
        analytic = dot(left, weights, ((1,), (1,)))
        real, imag = analytic[:, :count], analytic[:, count:]
        power = real * real + imag * imag + 1e-06
        envelope = power * lax.rsqrt(power)
        envelope_ref[chunk * CHUNK : (chunk + 1) * CHUNK, :] = envelope
        total = total + jnp.sum(envelope, axis=0, keepdims=True)
    scale = 1.0 / (total * (1.0 / SPAN))
    out_ref[...] = (envelope_ref[...] * scale - 1.0).astype(jnp.bfloat16)


def step_size(code):
    return jnp.exp2(code * 0.125) * (1.0 / LEVELS)


def encode(value):
    largest = jnp.max(jnp.abs(value), axis=1, keepdims=True)
    code = jnp.floor(8.0 * jnp.log2(jnp.maximum(largest, 1e-30))) + 1.0
    levels = jnp.round(value * (1.0 / step_size(code))).astype(jnp.int32)
    codes = jnp.broadcast_to(code, (value.shape[0], 128)).astype(jnp.int32)
    return jnp.concatenate([levels, codes], axis=1).astype(jnp.int16)


def decode(coded):
    columns = coded.shape[1] - 128
    code = coded[:, columns : columns + 1].astype(jnp.float32)
    return coded[:, :columns].astype(jnp.float32) * step_size(code)


def stack_kernel(offset, pieces, shifts_ref, *refs):
    functions_refs, extra_refs, (out_ref, sums_ref, near_ref) = refs[:pieces], refs[pieces:-3], refs[-3:]
    parts, count, nodes = shifts_ref.shape
    blocks = FINE // parts
    width = nodes // parts
    shifts = shifts_ref[offset]
    one = jnp.ones((), jnp.bfloat16)
    zero = jnp.zeros((), jnp.bfloat16)
    lagged = [ref[c * FINE : c * FINE + ROWS, :] for c in range(COARSE) for ref in functions_refs]
    lagged = jnp.concatenate(lagged, axis=1)

    def hot(coarse, block):
        lag = jnp.bfloat16(coarse * FINE + block * parts)
        return jnp.where(shifts == lag, one, zero)

    step = min(2, blocks)
    for first in range(0, blocks, step):
        rows = []
        for coarse in range(COARSE):
            rows.append(jnp.concatenate([hot(coarse, first + k) for k in range(step)], axis=1))
        columns = slice(first * nodes, (first + step) * nodes)
        sums_ref[:, columns] = dot(lagged, jnp.concatenate(rows, axis=0))
    for first, rows in ((0, ANCHORS), (ANCHORS, parts)):
        near = None
        for block in range(blocks):
            row = first + block * parts
            term = sums_ref[row : row + rows, block * nodes : (block + 1) * nodes]
            near = term if near is None else near + term
        near_ref[first : first + rows, :] = near
    lane = lax.broadcasted_iota(jnp.int32, (ANCHORS, nodes), 1) // width
    total = near_ref[:ANCHORS, :]
    for place in range(1, parts):
        total = jnp.where(lane == place, near_ref[place : place + ANCHORS, :], total)
    turned = total.T
    result = turned[:width]
    for place in range(1, parts):
        result = result + turned[place * width : (place + 1) * width]
    for ref in extra_refs:
        result = result + decode(ref[...])
    out_ref[...] = encode(result) if out_ref.dtype == jnp.int16 else result


def merge_kernel(sum_ref, arrived_ref, out_ref):
    out_ref[...] = encode(sum_ref[...] + decode(arrived_ref[...]))


def finish_kernel(scale, own_ref, first_ref, second_ref, out_ref):
    out_ref[...] = (own_ref[...] + decode(first_ref[...]) + decode(second_ref[...])) * scale


def exchange(value, axis, offset):
    size = lax.axis_size(axis)
    return lax.ppermute(value, axis, [(i, i ^ offset) for i in range(size)])


def gather_spectra(forward, records, axis, beside):
    size = lax.axis_size(axis)
    if size != 8:
        (spectrum,) = forward(records)
        return [[spectrum] + [exchange(spectrum, axis, offset) for offset in range(1, size)]], beside
    chip, own = forward(records, exchange(records, axis, 1))
    diagonal = exchange(own, axis, 6)
    near = lax.ppermute(chip, axis, [(i, i ^ (2 + 2 * (i & 1))) for i in range(size)])
    near, beside = lax.optimization_barrier((near, beside))
    return [[chip, near], [diagonal, exchange(near, axis, 1), exchange(diagonal, axis, 1)]], beside


def per_device(records, travel_p, travel_s):
    groups, sensors, nodes = travel_p.shape
    count = 2 * groups * sensors
    parts = lax.axis_size("sens")
    width = nodes // parts
    limit = pltpu.CompilerParams(vmem_limit_bytes=24 << 20)
    table = pl.pallas_call(
        table_kernel,
        out_shape=jax.ShapeDtypeStruct((2, 3, HALF, 2 * BAND), jnp.bfloat16),
        compiler_params=limit,
        cost_estimate=pl.CostEstimate(flops=16 * HALF * 4 * BAND, bytes_accessed=0, transcendentals=0),
    )()

    def forward(*blocks):
        sizes = [len(blocks) * sensors, sensors][: len(blocks)]
        return pl.pallas_call(
            forward_kernel,
            out_shape=[jax.ShapeDtypeStruct((size, 4 * BAND), jnp.float32) for size in sizes],
            compiler_params=limit,
        )(*blocks, table)

    shifts = pl.pallas_call(
        functools.partial(shift_kernel, "grid", "sens"),
        out_shape=jax.ShapeDtypeStruct((parts, count, nodes), jnp.bfloat16),
        scratch_shapes=[pltpu.VMEM((parts, count, nodes), jnp.float32)],
        compiler_params=limit,
        cost_estimate=pl.CostEstimate(
            flops=parts * parts * count * nodes, bytes_accessed=4 * count * nodes, transcendentals=0
        ),
    )(travel_p, travel_s)
    spectra, shifts = gather_spectra(forward, records[0], "grid", shifts)
    inverse = jnp.asarray(inverse_table())

    def rebuild(blocks):
        columns = 2 * sum(block.shape[0] for block in blocks)
        return pl.pallas_call(
            function_kernel,
            out_shape=jax.ShapeDtypeStruct((SPAN, columns), jnp.bfloat16),
            scratch_shapes=[pltpu.VMEM((SPAN, columns), jnp.float32)],
            compiler_params=pltpu.CompilerParams(vmem_limit_bytes=28 << 20),
            cost_estimate=pl.CostEstimate(
                flops=12 * SPAN * 2 * BAND * columns,
                bytes_accessed=2 * SPAN * columns,
                transcendentals=SPAN * columns,
            ),
        )(*blocks, inverse)

    functions = tuple(rebuild(blocks) for blocks in spectra)

    def stack(offset, code, *extra):
        plain = jax.ShapeDtypeStruct((width, ANCHORS), jnp.float32)
        coded = jax.ShapeDtypeStruct((width, ANCHORS + 128), jnp.int16)
        return pl.pallas_call(
            functools.partial(stack_kernel, offset, len(functions)),
            out_shape=coded if code else plain,
            scratch_shapes=[
                pltpu.VMEM((ROWS, FINE // parts * nodes), jnp.float32),
                pltpu.VMEM((ANCHORS + 8, nodes), jnp.float32),
            ],
            compiler_params=pltpu.CompilerParams(vmem_limit_bytes=28 << 20),
            cost_estimate=pl.CostEstimate(flops=1024, bytes_accessed=1024, transcendentals=0),
        )(shifts, *functions, *extra)

    sensor_total = sensors * lax.axis_size("grid") * parts
    scale = 1.0 / math.sqrt(2.0 * sensor_total)
    if parts == 4:
        far = stack(3, True)
        passing = exchange(far, "sens", 2)
        functions, far = lax.optimization_barrier((functions, far))
        across = stack(2, True)
        crossing = exchange(across, "sens", 2)
        functions, across = lax.optimization_barrier((functions, across))
        merged = pl.pallas_call(
            merge_kernel,
            out_shape=jax.ShapeDtypeStruct((width, ANCHORS + 128), jnp.int16),
            compiler_params=limit,
        )(stack(1, False), passing)
        nearby = exchange(merged, "sens", 1)
        functions, merged = lax.optimization_barrier((functions, merged))
        own = stack(0, False)
        return pl.pallas_call(
            functools.partial(finish_kernel, scale),
            out_shape=jax.ShapeDtypeStruct((width, ANCHORS), jnp.float32),
            compiler_params=limit,
        )(own, crossing, nearby)

    arrived = [exchange(stack(offset, False), "sens", offset) for offset in range(1, parts)]
    total = stack(0, False)
    for part in arrived:
        total = total + part
    return total * scale


def solution(mesh):
    return jax.shard_map(
        per_device,
        mesh=mesh,
        in_specs=(P("grid", "sens", None), P(None, "sens", "grid"), P(None, "sens", "grid")),
        out_specs=P(("grid", "sens"), None),
        check_vma=False,
    )
```

```python
import functools
import math

import jax
import jax.numpy as jnp
import ml_dtypes
import numpy as np
from jax import lax
from jax.experimental import pallas as pl
from jax.experimental.pallas import tpu as pltpu
from jax.sharding import PartitionSpec as P

NT = 2048
HALF = NT // 2
BAND = 128
P_LOW = 160
S_LOW = 48
LAGS = 64
ANCHORS = 1024
SPAN = 1088
FINE = 16
COARSE = LAGS // FINE
ROWS = ANCHORS + FINE
STEP = 32
LEVELS = 32000.0
CHUNKS = 2
CHUNK = SPAN // CHUNKS


def split_bf16(table, count):
    pieces = []
    rest = table.astype(np.float32)
    for _ in range(count):
        piece = rest.astype(ml_dtypes.bfloat16)
        pieces.append(piece)
        rest = rest - piece.astype(np.float32)
    return pieces


def inverse_table():
    times = np.arange(SPAN)
    columns = []
    for parity in (0, 1):
        bins = np.arange(parity, BAND, 2)
        angles = 2.0 * np.pi * ((times[:, None] * bins[None, :]) % NT) / NT
        columns += [np.cos(angles), np.sin(angles)]
    return np.concatenate(split_bf16(np.concatenate(columns, 1) * (2.0 / NT), 2), 1)


def split_value(value, count):
    pieces = []
    for _ in range(count):
        piece = value.astype(jnp.bfloat16)
        pieces.append(piece)
        value = value - piece.astype(jnp.float32)
    return pieces


def dot(a, b, contract=((1,), (0,))):
    return lax.dot_general(a, b, (contract, ((), ())), preferred_element_type=jnp.float32)


def group_order(size, here):
    if size != 8:
        return [here ^ offset for offset in range(size)]
    near = 2 + 2 * (here & 1)
    far = 6 - near
    mine = [here, here ^ 1, here ^ near, here ^ near ^ 1, here ^ 6]
    return mine + [here ^ 1 ^ far, here ^ far, here ^ 7]


def shift_kernel(axis, owner_axis, shift_p_ref, shift_s_ref, out_ref, turned_ref):
    groups, block, nodes = shift_p_ref.shape
    parts = out_ref.shape[0]
    width = nodes // parts
    order = group_order(groups, lax.axis_index(axis))
    halves = [order[:4], order[4:]] if groups == 8 else [order]
    refs = (shift_p_ref, shift_s_ref)
    rows = [ref[group] for half in halves for ref in refs for group in half]
    shifts = jnp.concatenate(rows, axis=0).astype(jnp.float32)
    lane = lax.broadcasted_iota(jnp.int32, shifts.shape, 1) // width
    for turn in range(parts):
        turned_ref[turn] = pltpu.roll(shifts, turn * width, 1) if turn else shifts
    owner = lax.axis_index(owner_axis)
    for offset in range(parts):
        target = owner ^ offset
        spread = turned_ref[(parts - target) & (parts - 1)]
        for place in range(1, parts):
            turned = turned_ref[(place - target) & (parts - 1)]
            spread = jnp.where(lane == place, turned, spread)
        out_ref[offset] = (spread - lane.astype(jnp.float32)).astype(jnp.bfloat16)


def table_kernel(table_ref):
    half = BAND // 2
    lane = lax.broadcasted_iota(jnp.int32, (STEP, BAND), 1)
    row = lax.broadcasted_iota(jnp.int32, (STEP, BAND), 0)
    bins = jnp.where(lane < half, P_LOW + 2 * lane, S_LOW + 2 * (lane - half))
    for parity in (0, 1):
        fine = ((row * (bins + parity)) & (NT - 1)).astype(jnp.float32) * (2.0 * math.pi / NT)
        base = ((row * STEP * (bins + parity)) & (NT - 1)).astype(jnp.float32) * (2.0 * math.pi / NT)
        fine_cos, fine_sin = jnp.cos(fine), jnp.sin(fine)
        base_cos, base_sin = jnp.cos(base), jnp.sin(base)
        for step in range(HALF // STEP):
            step_cos, step_sin = base_cos[step : step + 1], base_sin[step : step + 1]
            rows = slice(step * STEP, (step + 1) * STEP)
            for column, value in (
                (0, step_cos * fine_cos - step_sin * fine_sin),
                (BAND, step_sin * fine_cos + step_cos * fine_sin),
            ):
                for index, piece in enumerate(split_value(value, 3)):
                    table_ref[parity, index, rows, column : column + BAND] = piece


def forward_kernel(*refs):
    blocks = len(refs) // 2
    record_refs, table_ref, out_refs = refs[:blocks], refs[blocks], refs[blocks + 1 :]
    records = jnp.concatenate([ref[...] for ref in record_refs], axis=0)
    sensors = records.shape[0]
    half = BAND // 2
    early, late = records[:, :HALF], records[:, HALF:]
    for parity, folded in ((0, early + late), (1, early - late)):
        pieces = split_value(folded, 3)
        total = None
        for index in (2, 1, 0):
            stacked = jnp.concatenate(pieces[: 3 - index], axis=0)
            product = dot(stacked, table_ref[parity, index])
            for part in reversed(range(3 - index)):
                term = product[part * sensors : (part + 1) * sensors]
                total = term if total is None else total + term
        for band in range(2):
            column = (2 * band + parity) * BAND
            for side in range(2):
                first = side * BAND + band * half
                for ref in out_refs:
                    rows = ref.shape[0]
                    columns = slice(column + side * half, column + (side + 1) * half)
                    ref[:, columns] = total[:rows, first : first + half]


def function_kernel(*refs):
    spectrum_refs, (table_ref, out_ref, envelope_ref) = refs[:-3], refs[-3:]
    count = out_ref.shape[1]
    spectrum = jnp.concatenate([ref[...] for ref in spectrum_refs], axis=0)
    spectrum = jnp.concatenate([spectrum[:, : 2 * BAND], spectrum[:, 2 * BAND :]], axis=0)
    half = BAND // 2
    blocks = []
    for first in (0, BAND):
        block = pltpu.roll(spectrum[:, first : first + BAND], half, 1)
        lane = lax.broadcasted_iota(jnp.int32, block.shape, 1)
        blocks.append(jnp.where(lane < half, -block, block))
    spectrum = jnp.concatenate([spectrum, jnp.concatenate(blocks, axis=1)], axis=0)
    high, low = split_value(spectrum, 2)
    weights = jnp.concatenate([high, low, high], axis=1)
    total = jnp.zeros((1, count), jnp.float32)
    for chunk in range(CHUNKS):
        table = table_ref[chunk * CHUNK : (chunk + 1) * CHUNK, :]
        left = jnp.concatenate([table[:, : 2 * BAND], table], axis=1)
        analytic = dot(left, weights, ((1,), (1,)))
        real, imag = analytic[:, :count], analytic[:, count:]
        power = real * real + imag * imag + 1e-06
        envelope = power * lax.rsqrt(power)
        envelope_ref[chunk * CHUNK : (chunk + 1) * CHUNK, :] = envelope
        total = total + jnp.sum(envelope, axis=0, keepdims=True)
    scale = 1.0 / (total * (1.0 / SPAN))
    out_ref[...] = (envelope_ref[...] * scale - 1.0).astype(jnp.bfloat16)


def step_size(code):
    return jnp.exp2(code * 0.125) * (1.0 / LEVELS)


def encode(value):
    largest = jnp.max(jnp.abs(value), axis=1, keepdims=True)
    code = jnp.floor(8.0 * jnp.log2(jnp.maximum(largest, 1e-30))) + 1.0
    levels = jnp.round(value * (1.0 / step_size(code))).astype(jnp.int32)
    codes = jnp.broadcast_to(code, (value.shape[0], 128)).astype(jnp.int32)
    return jnp.concatenate([levels, codes], axis=1).astype(jnp.int16)


def decode(coded):
    columns = coded.shape[1] - 128
    code = coded[:, columns : columns + 1].astype(jnp.float32)
    return coded[:, :columns].astype(jnp.float32) * step_size(code)


def stack_kernel(offset, pieces, shifts_ref, *refs):
    functions_refs, extra_refs, (out_ref, sums_ref, near_ref) = refs[:pieces], refs[pieces:-3], refs[-3:]
    parts, count, nodes = shifts_ref.shape
    blocks = FINE // parts
    width = nodes // parts
    shifts = shifts_ref[offset]
    one = jnp.ones((), jnp.bfloat16)
    zero = jnp.zeros((), jnp.bfloat16)
    lagged = [ref[c * FINE : c * FINE + ROWS, :] for c in range(COARSE) for ref in functions_refs]
    lagged = jnp.concatenate(lagged, axis=1)

    def hot(coarse, block):
        lag = jnp.bfloat16(coarse * FINE + block * parts)
        return jnp.where(shifts == lag, one, zero)

    step = blocks
    for first in range(0, blocks, step):
        rows = []
        for coarse in range(COARSE):
            rows.append(jnp.concatenate([hot(coarse, first + k) for k in range(step)], axis=1))
        columns = slice(first * nodes, (first + step) * nodes)
        sums_ref[:, columns] = dot(lagged, jnp.concatenate(rows, axis=0))
    for first, rows in ((0, ANCHORS), (ANCHORS, parts)):
        near = None
        for block in range(blocks):
            row = first + block * parts
            term = sums_ref[row : row + rows, block * nodes : (block + 1) * nodes]
            near = term if near is None else near + term
        near_ref[first : first + rows, :] = near
    lane = lax.broadcasted_iota(jnp.int32, (ANCHORS, nodes), 1) // width
    total = near_ref[:ANCHORS, :]
    for place in range(1, parts):
        total = jnp.where(lane == place, near_ref[place : place + ANCHORS, :], total)
    turned = total.T
    result = turned[:width]
    for place in range(1, parts):
        result = result + turned[place * width : (place + 1) * width]
    for ref in extra_refs:
        result = result + decode(ref[...])
    out_ref[...] = encode(result) if out_ref.dtype == jnp.int16 else result


def merge_kernel(sum_ref, arrived_ref, out_ref):
    out_ref[...] = encode(sum_ref[...] + decode(arrived_ref[...]))


def finish_kernel(scale, own_ref, first_ref, second_ref, out_ref):
    out_ref[...] = (own_ref[...] + decode(first_ref[...]) + decode(second_ref[...])) * scale


def exchange(value, axis, offset):
    size = lax.axis_size(axis)
    return lax.ppermute(value, axis, [(i, i ^ offset) for i in range(size)])


def gather_spectra(forward, records, axis, beside):
    size = lax.axis_size(axis)
    if size != 8:
        (spectrum,) = forward(records)
        return [[spectrum] + [exchange(spectrum, axis, offset) for offset in range(1, size)]], beside
    chip, own = forward(records, exchange(records, axis, 1))
    diagonal = exchange(own, axis, 6)
    near = lax.ppermute(chip, axis, [(i, i ^ (2 + 2 * (i & 1))) for i in range(size)])
    near, beside = lax.optimization_barrier((near, beside))
    return [[chip, near], [diagonal, exchange(near, axis, 1), exchange(diagonal, axis, 1)]], beside


def per_device(records, travel_p, travel_s):
    groups, sensors, nodes = travel_p.shape
    count = 2 * groups * sensors
    parts = lax.axis_size("sens")
    width = nodes // parts
    limit = pltpu.CompilerParams(vmem_limit_bytes=24 << 20)
    table = pl.pallas_call(
        table_kernel,
        out_shape=jax.ShapeDtypeStruct((2, 3, HALF, 2 * BAND), jnp.bfloat16),
        compiler_params=limit,
        cost_estimate=pl.CostEstimate(flops=16 * HALF * 4 * BAND, bytes_accessed=0, transcendentals=0),
    )()

    def forward(*blocks):
        sizes = [len(blocks) * sensors, sensors][: len(blocks)]
        return pl.pallas_call(
            forward_kernel,
            out_shape=[jax.ShapeDtypeStruct((size, 4 * BAND), jnp.float32) for size in sizes],
            compiler_params=limit,
        )(*blocks, table)

    shifts = pl.pallas_call(
        functools.partial(shift_kernel, "grid", "sens"),
        out_shape=jax.ShapeDtypeStruct((parts, count, nodes), jnp.bfloat16),
        scratch_shapes=[pltpu.VMEM((parts, count, nodes), jnp.float32)],
        compiler_params=limit,
        cost_estimate=pl.CostEstimate(
            flops=parts * parts * count * nodes, bytes_accessed=4 * count * nodes, transcendentals=0
        ),
    )(travel_p, travel_s)
    spectra, shifts = gather_spectra(forward, records[0], "grid", shifts)
    inverse = jnp.asarray(inverse_table())

    def rebuild(blocks):
        columns = 2 * sum(block.shape[0] for block in blocks)
        return pl.pallas_call(
            function_kernel,
            out_shape=jax.ShapeDtypeStruct((SPAN, columns), jnp.bfloat16),
            scratch_shapes=[pltpu.VMEM((SPAN, columns), jnp.float32)],
            compiler_params=pltpu.CompilerParams(vmem_limit_bytes=28 << 20),
            cost_estimate=pl.CostEstimate(
                flops=12 * SPAN * 2 * BAND * columns,
                bytes_accessed=2 * SPAN * columns,
                transcendentals=SPAN * columns,
            ),
        )(*blocks, inverse)

    functions = tuple(rebuild(blocks) for blocks in spectra)

    def stack(offset, code, *extra):
        plain = jax.ShapeDtypeStruct((width, ANCHORS), jnp.float32)
        coded = jax.ShapeDtypeStruct((width, ANCHORS + 128), jnp.int16)
        return pl.pallas_call(
            functools.partial(stack_kernel, offset, len(functions)),
            out_shape=coded if code else plain,
            scratch_shapes=[
                pltpu.VMEM((ROWS, FINE // parts * nodes), jnp.float32),
                pltpu.VMEM((ANCHORS + 8, nodes), jnp.float32),
            ],
            compiler_params=pltpu.CompilerParams(vmem_limit_bytes=28 << 20),
            cost_estimate=pl.CostEstimate(flops=1024, bytes_accessed=1024, transcendentals=0),
        )(shifts, *functions, *extra)

    sensor_total = sensors * lax.axis_size("grid") * parts
    scale = 1.0 / math.sqrt(2.0 * sensor_total)
    if parts == 4:
        far = stack(3, True)
        passing = exchange(far, "sens", 2)
        functions, far = lax.optimization_barrier((functions, far))
        across = stack(2, True)
        crossing = exchange(across, "sens", 2)
        functions, across = lax.optimization_barrier((functions, across))
        merged = pl.pallas_call(
            merge_kernel,
            out_shape=jax.ShapeDtypeStruct((width, ANCHORS + 128), jnp.int16),
            compiler_params=limit,
        )(stack(1, False), passing)
        nearby = exchange(merged, "sens", 1)
        functions, merged = lax.optimization_barrier((functions, merged))
        own = stack(0, False)
        return pl.pallas_call(
            functools.partial(finish_kernel, scale),
            out_shape=jax.ShapeDtypeStruct((width, ANCHORS), jnp.float32),
            compiler_params=limit,
        )(own, crossing, nearby)

    arrived = [exchange(stack(offset, False), "sens", offset) for offset in range(1, parts)]
    total = stack(0, False)
    for part in arrived:
        total = total + part
    return total * scale


def solution(mesh):
    return jax.shard_map(
        per_device,
        mesh=mesh,
        in_specs=(P("grid", "sens", None), P(None, "sens", "grid"), P(None, "sens", "grid")),
        out_specs=P(("grid", "sens"), None),
        check_vma=False,
    )
```
